32 devices in a mesh: win: 4 (over y, x), lat: 8 (over z, core).
Axes of the slice: x: 2, y: 2, z: 4, core: 2. Of those that a mesh axis runs over, the one named last changes fastest.
Arguments:
- state: float32 [4, 1, 1024, 2048], P('win', None, 'lat'), may hold values from -6 to 6
- multipliers: float32 [4, 1, 1024, 2048], P('win', None, 'lat'), may hold values from -3 to 3
- observations: float32 [4, 2, 1, 1024, 2048], P('win', None, None, 'lat'), may hold values from -6 to 6
- obs_mask: int32 [4, 2, 1024, 2048], P('win', None, 'lat'), may hold values 0 or 1
- speed: float32 [1], replicated, may hold values from 0.1 to 0.3
- drift: float32 [1], replicated, may hold values from 0.1 to 0.4
- kappa: float32 [1], replicated, may hold values from 0.05 to 0.2
- lat_spectrum: float32 [1, 1024], replicated, may hold values from 0.05 to 1
- lon_spectrum: float32 [1, 2048], replicated, may hold values from 0.05 to 1
Outputs:
- new_state: float32 [4, 1, 1024, 2048], P('win', None, 'lat')
- new_multipliers: float32 [4, 1, 1024, 2048], P('win', None, 'lat')
The draws below stay inside these ranges and needn't reach their ends.
All inputs are finite; a program needn't handle non-finite values. No bound on the sum of `obs_mask` on one device may be relied on, other than what follows from the above.
Results may differ from the reference program's by a relative error of at most 0.0001.
Values sent between devices are 32-bit elements; how exact they have to be, the bound alone decides.
No kernel may reach another device: no remote copies, remote signals or barrier semaphores. Data moves between devices by JAX's collectives and lax.ppermute only.
A program may use at most 64 MiB of HBM per device.

```python
import math
import jax
import jax.numpy as jnp
from jax import lax

NLON = 2048
NLAT = 1024
LEV = 1
STEPS = 2
ITERS = 1
NWIN = 4


def place_ends(drawn, rng, smallest, top_value):
    shape = drawn.shape
    index_at = [jax.random.randint(jax.random.fold_in(rng, axis), (), 0, shape[axis]) for axis in range(len(shape))]
    drawn = drawn.at[tuple(index_at)].set(smallest)
    longest = shape.index(max(shape))
    index_at[longest] = (index_at[longest] + 1) % shape[longest]
    return drawn.at[tuple(index_at)].set(top_value)


def levels(own_key, dims, split, least, high):
    loudness = 1.0
    for axis_at, parts in split:
        draws = jax.random.uniform(jax.random.fold_in(jax.random.fold_in(own_key, 6), axis_at), (parts,), jnp.float32, least / len(split), high / len(split))
        loudness = loudness * jnp.repeat(jnp.exp(draws), dims[axis_at] // parts).reshape((-1,) + (1,) * (len(dims) - 1 - axis_at))
    return loudness


def bell_draw(own_key, extent, deviation, limit, pieces=(), held_as=jnp.bfloat16):
    values = jax.random.normal(own_key, extent, jnp.float32) * deviation
    if len(pieces) > 0:
        values = levels(own_key, extent, pieces, -0.22, 0.18) * values
    return jnp.clip(values, min=-limit, max=limit).astype(held_as)


def setup_inputs(seed: int = 0) -> dict:
    arg_keys = jax.random.split(jax.random.key(seed), 10)
    state = bell_draw(arg_keys[0], (NWIN, LEV, NLAT, NLON), 1.0, 6.0, ((0, 4), (2, 8)), jnp.float32)
    multipliers = bell_draw(arg_keys[1], (NWIN, LEV, NLAT, NLON), 0.5, 3.0, ((0, 4), (2, 8)), jnp.float32)
    observations = bell_draw(arg_keys[2], (NWIN, STEPS, LEV, NLAT, NLON), 1.0, 6.0, ((0, 4), (3, 8)), jnp.float32)
    obs_mask = place_ends((jax.random.randint(arg_keys[3], (NWIN, STEPS, NLAT, NLON), 0, 3) < 1).astype(jnp.int32), jax.random.fold_in(arg_keys[3], 1), 0, 1)
    speed = jnp.clip(jax.random.uniform(arg_keys[4], (LEV,), jnp.float32, 0.1, 0.3), 0.1, 0.3)
    drift = jnp.clip(jax.random.uniform(arg_keys[5], (LEV,), jnp.float32, 0.1, 0.4), 0.1, 0.4)
    kappa = jnp.clip(jax.random.uniform(arg_keys[6], (LEV,), jnp.float32, 0.05, 0.2), 0.05, 0.2)
    lat_spectrum = jnp.clip(jnp.exp(jax.random.uniform(arg_keys[7], (LEV, NLAT), jnp.float32, math.log(0.05), math.log(1.0))), 0.05, 1.0)
    lon_spectrum = jnp.clip(jnp.exp(jax.random.uniform(arg_keys[8], (LEV, NLON), jnp.float32, math.log(0.05), math.log(1.0))), 0.05, 1.0)
    return {"state": state, "multipliers": multipliers, "observations": observations, "obs_mask": obs_mask, "speed": speed, "drift": drift, "kappa": kappa, "lat_spectrum": lat_spectrum, "lon_spectrum": lon_spectrum}


def hartley(count):
    index = jnp.arange(count, dtype=jnp.int32)
    product = (index[:, None] * index[None, :]) % count
    angle = product.astype(jnp.float32) * (2.0 * math.pi / count)
    return jnp.cos(angle) + jnp.sin(angle)


def advance(field, speed, drift, kappa):
    east = jnp.roll(field, -1, axis=-1)
    west = jnp.roll(field, 1, axis=-1)
    widths = [(0, 0)] * (field.ndim - 2) + [(1, 1), (0, 0)]
    padded = jnp.pad(field, widths)
    north = padded[..., 2:, :]
    south = padded[..., :-2, :]
    speed_c = speed[:, None, None]
    drift_c = drift[:, None, None]
    kappa_c = kappa[:, None, None]
    return (field - speed_c * field * (east - west) * 0.5 - drift_c * (north - south) * 0.5
            + kappa_c * (east + west + north + south - 4.0 * field))


def reference(state, multipliers, observations, obs_mask, speed, drift, kappa, lat_spectrum, lon_spectrum):
    high = lax.Precision.HIGHEST
    h_lon = hartley(NLON)
    h_lat = hartley(NLAT)
    weight = lat_spectrum[:, :, None] * lon_spectrum[:, None, :]
    mask = obs_mask.astype(jnp.float32)

    def covariance(resid):
        spectral = jnp.matmul(resid, h_lon, precision=high)
        spectral = jnp.einsum('ij,ljk->lik', h_lat, spectral, precision=high) * weight
        spectral = jnp.einsum('ij,ljk->lik', h_lat, spectral, precision=high)
        return jnp.matmul(spectral, h_lon, precision=high) / (NLAT * NLON)

    windows = jnp.arange(NWIN, dtype=jnp.int32)[:, None, None, None]
    field = state
    lam = multipliers
    for loop_index in range(ITERS):
        first = advance(field, speed, drift, kappa)
        second = advance(first, speed, drift, kappa)
        defect = (mask[:, 0][:, None] * (observations[:, 0] - first)
                  + mask[:, 1][:, None] * (observations[:, 1] - second))
        prior_end = jnp.concatenate([jnp.zeros_like(second[:1]), second[:-1]], axis=0)
        mismatch = jnp.where(windows > 0, field - prior_end, jnp.float32(0.0))
        lam = lam + 0.5 * mismatch
        summed = jnp.cumsum(lam, axis=0)
        carried = jnp.concatenate([jnp.zeros_like(lam[:1]), summed[:-1]], axis=0)
        resid = defect + lam - carried / jnp.maximum(windows, 1).astype(jnp.float32)
        field = field + 0.5 * lax.map(covariance, resid)
    return field, lam
```

```python
import functools
import math

import numpy as np
import jax
import jax.numpy as jnp
from jax import lax
from jax.experimental import pallas as pl
from jax.experimental.pallas import tpu as pltpu
from jax.sharding import PartitionSpec as P


LANES = 128
VMEM = pl.BlockSpec(memory_space=pltpu.VMEM)
SMEM = pl.BlockSpec(memory_space=pltpu.SMEM)

def trig_tables(count):
    low = count // LANES
    blocks = low // 2
    turn = 2.0 * math.pi
    fine = np.arange(LANES)
    coarse = np.arange(low)
    inner = turn * ((fine[:, None] * fine[None, :]) % LANES) / LANES
    twist = turn * (coarse[:, None] * fine[None, :]) / count
    outer = turn * ((np.arange(blocks)[:, None] * coarse[None, :]) % low) / low
    even = (coarse % 2 == 0)[None, :]
    keep = np.concatenate([np.broadcast_to(even, outer.shape), np.broadcast_to(~even, outer.shape)])
    outer = np.concatenate([outer, outer])
    pack = lambda angle, scale: np.concatenate([np.cos(angle), np.sin(angle)], axis=1) * scale
    return (pack(inner, 1.0).astype(np.float32), pack(twist, 1.0 / count).astype(np.float32),
            (np.cos(outer) * keep).astype(np.float32), (np.sin(outer) * keep).astype(np.float32))

def build_kernel(count, d_ref, inner_ref, twist_ref, cos_ref, sin_ref, even_hi, even_lo, odd_hi, odd_lo, toep, hank):
    blocks = count // LANES // 2
    high = lax.Precision.HIGHEST
    mm = functools.partial(jnp.dot, precision=high, preferred_element_type=jnp.float32)
    g = lax.dot_general(d_ref[...], inner_ref[...], (((0,), (0,)), ((), ())), precision=high,
                        preferred_element_type=jnp.float32)
    gc, gs = g[:, :LANES], g[:, LANES:]
    tc, ts = twist_ref[:, :LANES], twist_ref[:, LANES:]
    gc, gs = gc * tc - gs * ts, gc * ts + gs * tc
    c = mm(cos_ref[...], gc) - mm(sin_ref[...], gs)
    s = mm(sin_ref[...], gc) + mm(cos_ref[...], gs)
    rows = lax.broadcasted_iota(jnp.int32, (LANES, LANES), 0)
    cols = lax.broadcasted_iota(jnp.int32, (LANES, LANES), 1)
    flip = jnp.where(rows + cols == LANES - 1, 1.0, 0.0)
    for part in range(2):
        wrap = 1.0 if part == 0 else -1.0
        hi_ref, lo_ref = (even_hi, even_lo) if part == 0 else (odd_hi, odd_lo)
        def row(table, at):
            sign = 1.0
            if at < 0 or at >= blocks:
                sign, at = wrap, at % blocks
            at += part * blocks
            return sign * table[at:at + 1]
        for b in range(blocks):
            window = jnp.concatenate([row(c, b - 1), row(c, b)], axis=1)
            window = jnp.broadcast_to(window, (LANES, 2 * LANES))
            toep[b] = pltpu.roll(window, 0, 1, stride=1, stride_axis=0)[:, LANES:]
            window = jnp.concatenate([row(s, b), row(s, b + 1)], axis=1)
            window = jnp.broadcast_to(window, (LANES, 2 * LANES))
            window = pltpu.roll(window, LANES + 1, 1, stride=1, stride_axis=0)[:, :LANES]
            hank[b] = mm(flip, window)
        def body(i, _):
            for j in range(blocks):
                t = toep[lax.rem(j - i + blocks, blocks)]
                h = hank[lax.rem(i + j, blocks)]
                if part == 1:
                    t = t * jnp.where(j < i, -1.0, 1.0)
                    h = h * jnp.where(i + j >= blocks, -1.0, 1.0)
                a = t + h
                hi = a.astype(jnp.bfloat16)
                at = (pl.ds(pl.multiple_of(i * LANES, LANES), LANES), pl.ds(j * LANES, LANES))
                hi_ref[at] = hi
                lo_ref[at] = (a - hi.astype(jnp.float32)).astype(jnp.bfloat16)
            return 0
        lax.fori_loop(0, blocks, body, 0)

def build(spectrum):
    count = spectrum.shape[0]
    half = count // 2
    tables = trig_tables(count)
    shape = jax.ShapeDtypeStruct((half, half), jnp.bfloat16)
    return pl.pallas_call(
        functools.partial(build_kernel, count),
        out_shape=[shape] * 4, in_specs=[VMEM] * 5, out_specs=[VMEM] * 4,
        scratch_shapes=[pltpu.VMEM((half // LANES, LANES, LANES), jnp.float32)] * 2,
        cost_estimate=pl.CostEstimate(flops=2 * half * half * 8, bytes_accessed=8 * half * half, transcendentals=0),
        name="build%d" % count,
    )(spectrum.reshape(LANES, count // LANES), *tables)


def extended(block, sides, width):
    for axis, dim in sides:
        count = lax.axis_size(axis)
        forward = [(i, i + 1) for i in range(count - 1)]
        backward = [(target, source) for source, target in forward]
        low = lax.ppermute(
            lax.slice_in_dim(block, block.shape[dim] - width, None, axis=dim), axis, forward
        )
        high = lax.ppermute(lax.slice_in_dim(block, 0, width, axis=dim), axis, backward)
        block = jnp.concatenate([low, block, high], axis=dim)
    return block


def passed_along(value, axis, steps):
    count = lax.axis_size(axis)
    first, last = (max(0, -steps), min(count, count - steps))
    return lax.ppermute(value, axis, [(source, source + steps) for source in range(first, last)])


def prefix(array, axis, combine, identity):
    peers, here = (lax.axis_size(axis), lax.axis_index(axis))
    everything = lax.all_gather(array, axis)
    start = jnp.broadcast_to(jnp.asarray(identity, array.dtype), array.shape)

    def turn(k, before):
        reached = k < here
        new = combine(before, everything[k])
        return jnp.where(reached, new, before)

    return lax.fori_loop(0, peers, turn, start)


def hartley(count):
    index = jnp.arange(count, dtype=jnp.int32)
    product = index[:, None] * index[None, :] % count
    angle = product.astype(jnp.float32) * (2.0 * math.pi / count)
    return jnp.cos(angle) + jnp.sin(angle)


def advance(padded, speed, drift, kappa):
    field = padded[:, 1:-1]
    north = padded[:, 2:]
    south = padded[:, :-2]
    east = jnp.roll(field, -1, axis=-1)
    west = jnp.roll(field, 1, axis=-1)
    speed_c = speed[:, None, None]
    drift_c = drift[:, None, None]
    kappa_c = kappa[:, None, None]
    return (
        field
        - speed_c * field * (east - west) * 0.5
        - drift_c * (north - south) * 0.5
        + kappa_c * (east + west + north + south - 4.0 * field)
    )


def per_device_any(
    state, multipliers, observations, obs_mask, speed, drift, kappa, lat_spectrum, lon_spectrum
):
    high = lax.Precision.HIGHEST
    field = state[0]
    lam = multipliers[0]
    observed = observations[0]
    mask = obs_mask[0].astype(jnp.float32)
    band = field.shape[1]
    nlon = field.shape[2]
    bands = lax.axis_size("lat")
    nlat = band * bands
    columns = nlon // bands
    lat_index = lax.axis_index("lat")
    win_index = lax.axis_index("win")
    h_lon = hartley(nlon)
    h_lat = hartley(nlat)
    lon_part = lax.dynamic_slice_in_dim(lon_spectrum, lat_index * columns, columns, 1)
    weight = lat_spectrum[:, :, None] * lon_part[:, None, :]
    divisor = jnp.maximum(win_index, 1).astype(jnp.float32)
    rows_global = lat_index * band + jnp.arange(-1, band + 1, dtype=jnp.int32)
    inside = ((rows_global >= 0) & (rows_global < nlat))[None, :, None]
    padded = extended(field, (("lat", 1),), 2)
    widened = advance(padded, speed, drift, kappa)
    widened = jnp.where(inside, widened, jnp.float32(0.0))
    first = widened[:, 1:-1]
    second = advance(widened, speed, drift, kappa)
    defect = mask[0][None] * (observed[0] - first) + mask[1][None] * (observed[1] - second)
    prior_end = passed_along(second, "win", 1)
    mismatch = jnp.where(win_index > 0, field - prior_end, jnp.float32(0.0))
    lam = lam + 0.5 * mismatch
    carried = prefix(lam, "win", lambda earlier, later: earlier + later, jnp.zeros_like(lam))
    resid = defect + lam - carried / divisor
    spectral = jnp.matmul(resid, h_lon, precision=high)
    spectral = lax.all_to_all(spectral, "lat", split_axis=2, concat_axis=1, tiled=True)
    spectral = jnp.einsum("ij,ljk->lik", h_lat, spectral, precision=high) * weight
    spectral = jnp.einsum("ij,ljk->lik", h_lat, spectral, precision=high)
    spectral = lax.all_to_all(spectral, "lat", split_axis=1, concat_axis=2, tiled=True)
    increment = jnp.matmul(spectral, h_lon, precision=high) / (nlat * nlon)
    field = field + 0.5 * increment
    return (field[None], lam[None])


def split(value):
    hi = value.astype(jnp.bfloat16)
    return hi, (value - hi.astype(jnp.float32)).astype(jnp.bfloat16)


def lat_kernel(bands, here_ref, *refs):
    blocks, (ehi, elo, ohi, olo) = refs[:bands], refs[bands:bands + 4]
    outs, (gathered, mixed) = refs[bands + 4:2 * bands + 4], refs[2 * bands + 4:]
    here = here_ref[0]
    pairs = bands // 2
    band, columns = blocks[0].shape
    for shift in range(pairs):
        source = lax.rem(here - shift + bands, bands)
        rows = pl.ds(pl.multiple_of(lax.rem(source, pairs) * band, band), band)
        first, other = blocks[shift][...], blocks[shift + pairs][...]
        sign = jnp.where(source < pairs, 1.0, -1.0)
        for part, value in enumerate((first + other, (first - other) * sign)):
            hi, lo = split(value)
            gathered[part, rows, :columns] = hi
            gathered[part, rows, columns:] = lo
    dot = functools.partial(jnp.dot, preferred_element_type=jnp.float32)
    for part, (hi, lo) in enumerate(((ehi, elo), (ohi, olo))):
        both = dot(hi[...], gathered[part])
        mixed[part] = both[:, :columns] + both[:, columns:] + dot(lo[...], gathered[part, :, :columns])
    for shift in range(bands):
        target = lax.rem(here + shift, bands)
        rows = pl.ds(pl.multiple_of(lax.rem(target, pairs) * band, band), band)
        sign = jnp.where(target < pairs, 1.0, -1.0)
        outs[shift][...] = mixed[0, rows] + sign * mixed[1, rows]


def lat_apply(here, blocks, matrices):
    bands = len(blocks)
    band, columns = blocks[0].shape
    half = matrices[0].shape[0]
    return pl.pallas_call(
        functools.partial(lat_kernel, bands),
        out_shape=[jax.ShapeDtypeStruct((band, columns), jnp.float32)] * bands,
        in_specs=[SMEM] + [VMEM] * (bands + 4),
        out_specs=[VMEM] * bands,
        scratch_shapes=[
            pltpu.VMEM((2, half, 2 * columns), jnp.bfloat16),
            pltpu.VMEM((2, half, columns), jnp.float32),
        ],
        cost_estimate=pl.CostEstimate(
            flops=12 * half * half * columns, bytes_accessed=8 * half * half, transcendentals=0
        ),
        name="lat_apply",
    )(here, *blocks, *matrices)


def gather_rows(here, bands, blocks, gathered):
    band, columns = blocks[0].shape
    for shift in range(bands):
        source = lax.rem(here - shift + bands, bands)
        at = pl.ds(pl.multiple_of(source * columns, columns), columns)
        hi, lo = split(blocks[shift][...])
        gathered[:band, at] = hi
        gathered[band:, at] = lo


def lon_product(band, hi, lo, gathered):
    dot = functools.partial(jnp.dot, preferred_element_type=jnp.float32)
    both = dot(gathered[...], hi[...])
    return both[:band] + both[band:] + dot(gathered[:band], lo[...])


def lon_even_kernel(bands, here_ref, *refs):
    blocks, (hi, lo, out, gathered) = refs[:bands], refs[bands:]
    gather_rows(here_ref[0], bands, blocks, gathered)
    out[...] = lon_product(blocks[0].shape[0], hi, lo, gathered)


def lon_odd_kernel(bands, here_ref, *refs):
    blocks, (hi, lo, even, field, out, gathered) = refs[:bands], refs[bands:]
    gather_rows(here_ref[0], bands, blocks, gathered)
    half = hi.shape[0]
    odd = lon_product(blocks[0].shape[0], hi, lo, gathered)
    out[:, :half] = field[:, :half] + 0.5 * (even[...] + odd)
    out[:, half:] = field[:, half:] + 0.5 * (even[...] - odd)


def lon_apply(here, blocks, matrices, extra=()):
    bands = len(blocks)
    band, columns = blocks[0].shape
    half = matrices[0].shape[0]
    return pl.pallas_call(
        functools.partial(lon_odd_kernel if extra else lon_even_kernel, bands),
        out_shape=jax.ShapeDtypeStruct((band, 2 * half if extra else half), jnp.float32),
        in_specs=[SMEM] + [VMEM] * (bands + 2 + len(extra)),
        out_specs=VMEM,
        scratch_shapes=[pltpu.VMEM((2 * band, half), jnp.bfloat16)],
        cost_estimate=pl.CostEstimate(
            flops=6 * band * half * half, bytes_accessed=4 * half * half, transcendentals=0
        ),
        name="lon_apply",
    )(here, *blocks, *matrices, *extra)


def exchange(blocks):
    bands = len(blocks)
    moved = [blocks[0]]
    for shift in range(1, bands):
        route = [(source, (source + shift) % bands) for source in range(bands)]
        moved.append(lax.ppermute(blocks[shift], "lat", route))
    return moved


def halves(value):
    half = value.shape[1] // 2
    left, right = value[:, :half], value[:, half:]
    return left + right, left - right


def joined(plus, minus):
    return jnp.concatenate([0.5 * (plus + minus), 0.5 * (plus - minus)], axis=1)


def per_device(
    state, multipliers, observations, obs_mask, speed, drift, kappa, lat_spectrum, lon_spectrum
):
    bands, windows = lax.axis_size("lat"), lax.axis_size("win")
    band, nlon = state.shape[2:]
    columns = nlon // 2 // bands
    if windows != 4 or state.shape[1] != 1 or bands % 2 or band % LANES or columns % LANES:
        return per_device_any(
            state, multipliers, observations, obs_mask, speed, drift, kappa, lat_spectrum, lon_spectrum
        )
    lat_index, win_index = lax.axis_index("lat"), lax.axis_index("win")
    here = lat_index.astype(jnp.int32).reshape(1)
    lat_matrices = build(lat_spectrum[0])
    lon_matrices = build(lon_spectrum[0])
    field = state[0]
    mask = obs_mask[0].astype(jnp.float32)
    rows_global = lat_index * band + jnp.arange(-1, band + 1, dtype=jnp.int32)
    inside = ((rows_global >= 0) & (rows_global < band * bands))[None, :, None]
    padded = extended(field, (("lat", 1),), 2)
    widened = jnp.where(inside, advance(padded, speed, drift, kappa), jnp.float32(0.0))
    second = advance(widened, speed, drift, kappa)[0]
    first = widened[0, 1:-1]
    field = field[0]
    ended = 0.5 * second
    own = multipliers[0, 0] + jnp.where(win_index > 0, 0.5 * field, jnp.float32(0.0))
    defect = mask[0] * (observations[0, 0, 0] - first) + mask[1] * (observations[0, 1, 0] - second)
    base = halves(defect + own)
    step = own - ended
    send = ended + own / (win_index + 1).astype(jnp.float32)
    step, send = halves(step), halves(send)
    is_first, is_second, is_last = win_index == 0, win_index == 1, win_index == 3
    parts, got = [], []
    for part in range(2):
        outgoing = jnp.where(is_first, step[part], send[part])
        near = lax.ppermute(outgoing, "win", [(0, 1), (1, 0), (2, 3)])
        direct = lax.ppermute(send[part], "win", [(0, 1)])
        onward = near + jnp.where(is_first, 0.5, 1.0) * step[part]
        far = lax.ppermute(onward, "win", [(0, 2), (1, 3)])
        resid = (
            base[part] - jnp.where(is_last, 1.0, 0.0) * near - direct
            - jnp.where(is_last, 1.0 / 3.0, 1.0) * far
        )
        got.append((near, direct))
        blocks = []
        for shift in range(bands):
            target = lax.rem(lat_index + shift, bands)
            blocks.append(lax.dynamic_slice_in_dim(resid, target * columns, columns, 1))
        parts.append(blocks)
    later = lax.ppermute(ended, "win", [(1, 2), (2, 3)])
    mid = [lat_apply(here, exchange(blocks), lat_matrices) for blocks in parts]
    back = [exchange(blocks) for blocks in mid]
    even = lon_apply(here, back[0], lon_matrices[:2])
    field = lon_apply(here, back[1], lon_matrices[2:], (even, field))
    near, direct = (joined(got[0][at], got[1][at]) for at in range(2))
    lam = own - jnp.where(is_second, 0.5 * (direct - near), later)
    return (field[None, None], lam[None, None])


def solution(mesh):
    return jax.shard_map(
        per_device,
        mesh=mesh,
        in_specs=(
            P("win", None, "lat", None),
            P("win", None, "lat", None),
            P("win", None, None, "lat", None),
            P("win", None, "lat", None),
            P(),
            P(),
            P(),
            P(),
            P(),
        ),
        out_specs=(P("win", None, "lat", None), P("win", None, "lat", None)),
        check_vma=False,
    )
```

```python
import functools
import math

import numpy as np
import jax
import jax.numpy as jnp
from jax import lax
from jax.experimental import pallas as pl
from jax.experimental.pallas import tpu as pltpu
from jax.sharding import PartitionSpec as P


LANES = 128
ROWS = 8
VMEM = pl.BlockSpec(memory_space=pltpu.VMEM)
SMEM = pl.BlockSpec(memory_space=pltpu.SMEM)
ANY = pl.BlockSpec(memory_space=pl.ANY)
LIMIT = pltpu.CompilerParams(vmem_limit_bytes=16 * 2**20)


def trig_tables(count):
    low = count // LANES
    blocks = low // 2
    turn = 2.0 * math.pi
    fine = np.arange(LANES)
    coarse = np.arange(low)
    inner = turn * ((coarse[:, None] * fine[None, :]) % low) / low
    middle = turn * (((fine // low)[:, None] * fine[None, :]) % LANES) / LANES
    member = (coarse[:, None] == (fine % low)[None, :]).astype(np.float32)
    twist = turn * (coarse[:, None] * fine[None, :]) / count
    outer = turn * ((np.arange(blocks)[:, None] * coarse[None, :]) % low) / low
    even = (coarse % 2 == 0)[None, :]
    keep = np.concatenate([np.broadcast_to(even, outer.shape), np.broadcast_to(~even, outer.shape)])
    outer = np.concatenate([outer, outer])
    pack = lambda angle, scale: np.concatenate([np.cos(angle), np.sin(angle)], axis=1) * scale
    return (pack(inner, 1.0).astype(np.float32), pack(middle, 1.0).astype(np.float32), member, pack(twist, 1.0 / count).astype(np.float32),
            (np.cos(outer) * keep).astype(np.float32), (np.sin(outer) * keep).astype(np.float32))


def build_kernel(count, d_ref, inner_ref, middle_ref, member_ref, twist_ref, cos_ref, sin_ref, even_hi, even_lo, odd_hi, odd_lo, toep, hank):
    blocks = count // LANES // 2
    high = lax.Precision.HIGHEST
    mm = functools.partial(jnp.dot, precision=high, preferred_element_type=jnp.float32)

    def turned(value, table):
        real, imag = value[:, :LANES], value[:, LANES:]
        tc, ts = table[:, :LANES], table[:, LANES:]
        return jnp.concatenate([real * tc - imag * ts, real * ts + imag * tc], axis=1)

    spectrum = jnp.concatenate([d_ref[:, at:at + LANES] for at in range(0, count, LANES)], axis=0)
    g = lax.dot_general(spectrum, inner_ref[...], (((0,), (0,)), ((), ())), precision=high,
                        preferred_element_type=jnp.float32)
    g = turned(mm(member_ref[...], turned(g, middle_ref)), twist_ref)
    gc, gs = g[:, :LANES], g[:, LANES:]
    c = mm(cos_ref[...], gc) - mm(sin_ref[...], gs)
    s = mm(sin_ref[...], gc) + mm(cos_ref[...], gs)
    rows = lax.broadcasted_iota(jnp.int32, (LANES, LANES), 0)
    cols = lax.broadcasted_iota(jnp.int32, (LANES, LANES), 1)
    flip = jnp.where(rows + cols == LANES - 1, 1.0, 0.0)
    for part in range(2):
        wrap = 1.0 if part == 0 else -1.0
        hi_ref, lo_ref = (even_hi, even_lo) if part == 0 else (odd_hi, odd_lo)

        def row(table, at):
            sign = 1.0
            if at < 0 or at >= blocks:
                sign, at = wrap, at % blocks
            at += part * blocks
            return sign * table[at:at + 1]

        for b in range(blocks):
            window = jnp.concatenate([row(c, b - 1), row(c, b)], axis=1)
            window = jnp.broadcast_to(window, (LANES, 2 * LANES))
            toep[b] = pltpu.roll(window, 0, 1, stride=1, stride_axis=0)[:, LANES:]
            window = jnp.concatenate([row(s, b), row(s, b + 1)], axis=1)
            window = jnp.broadcast_to(window, (LANES, 2 * LANES))
            window = pltpu.roll(window, LANES + 1, 1, stride=1, stride_axis=0)[:, :LANES]
            hank[b] = mm(flip, window)

        def body(i, _):
            for j in range(blocks):
                t = toep[lax.rem(j - i + blocks, blocks)]
                h = hank[lax.rem(i + j, blocks)]
                if part == 1:
                    t = t * jnp.where(j < i, -1.0, 1.0)
                    h = h * jnp.where(i + j >= blocks, -1.0, 1.0)
                a = t + h
                hi = a.astype(jnp.bfloat16)
                at = (pl.ds(pl.multiple_of(i * LANES, LANES), LANES), pl.ds(j * LANES, LANES))
                hi_ref[at] = hi
                lo_ref[at] = (a - hi.astype(jnp.float32)).astype(jnp.bfloat16)
            return 0

        lax.fori_loop(0, blocks, body, 0)


def build(spectrum):
    count = spectrum.shape[1]
    half = count // 2
    tables = trig_tables(count)
    shape = jax.ShapeDtypeStruct((half, half), jnp.bfloat16)
    return pl.pallas_call(
        functools.partial(build_kernel, count),
        out_shape=[shape] * 4, in_specs=[VMEM] * 7, out_specs=[VMEM] * 4,
        scratch_shapes=[pltpu.VMEM((half // LANES, LANES, LANES), jnp.float32)] * 2,
        compiler_params=LIMIT,
        cost_estimate=pl.CostEstimate(flops=2 * half * half * 8, bytes_accessed=8 * half * half, transcendentals=0),
    )(spectrum, *tables)


def extended(block, sides, width):
    for axis, dim in sides:
        count = lax.axis_size(axis)
        forward = [(i, i + 1) for i in range(count - 1)]
        backward = [(target, source) for source, target in forward]
        low = lax.ppermute(
            lax.slice_in_dim(block, block.shape[dim] - width, None, axis=dim), axis, forward
        )
        high = lax.ppermute(lax.slice_in_dim(block, 0, width, axis=dim), axis, backward)
        block = jnp.concatenate([low, block, high], axis=dim)
    return block


def passed_along(value, axis, steps):
    count = lax.axis_size(axis)
    first, last = (max(0, -steps), min(count, count - steps))
    return lax.ppermute(value, axis, [(source, source + steps) for source in range(first, last)])


def prefix(array, axis, combine, identity):
    peers, here = (lax.axis_size(axis), lax.axis_index(axis))
    everything = lax.all_gather(array, axis)
    start = jnp.broadcast_to(jnp.asarray(identity, array.dtype), array.shape)

    def turn(k, before):
        reached = k < here
        new = combine(before, everything[k])
        return jnp.where(reached, new, before)

    return lax.fori_loop(0, peers, turn, start)


def hartley(count):
    index = jnp.arange(count, dtype=jnp.int32)
    product = index[:, None] * index[None, :] % count
    angle = product.astype(jnp.float32) * (2.0 * math.pi / count)
    return jnp.cos(angle) + jnp.sin(angle)


def advance(padded, speed, drift, kappa):
    field = padded[:, 1:-1]
    north = padded[:, 2:]
    south = padded[:, :-2]
    east = jnp.roll(field, -1, axis=-1)
    west = jnp.roll(field, 1, axis=-1)
    speed_c = speed[:, None, None]
    drift_c = drift[:, None, None]
    kappa_c = kappa[:, None, None]
    return (
        field
        - speed_c * field * (east - west) * 0.5
        - drift_c * (north - south) * 0.5
        + kappa_c * (east + west + north + south - 4.0 * field)
    )


def per_device_any(
    state, multipliers, observations, obs_mask, speed, drift, kappa, lat_spectrum, lon_spectrum
):
    high = lax.Precision.HIGHEST
    field = state[0]
    lam = multipliers[0]
    observed = observations[0]
    mask = obs_mask[0].astype(jnp.float32)
    band = field.shape[1]
    nlon = field.shape[2]
    bands = lax.axis_size("lat")
    nlat = band * bands
    columns = nlon // bands
    lat_index = lax.axis_index("lat")
    win_index = lax.axis_index("win")
    h_lon = hartley(nlon)
    h_lat = hartley(nlat)
    lon_part = lax.dynamic_slice_in_dim(lon_spectrum, lat_index * columns, columns, 1)
    weight = lat_spectrum[:, :, None] * lon_part[:, None, :]
    divisor = jnp.maximum(win_index, 1).astype(jnp.float32)
    rows_global = lat_index * band + jnp.arange(-1, band + 1, dtype=jnp.int32)
    inside = ((rows_global >= 0) & (rows_global < nlat))[None, :, None]
    padded = extended(field, (("lat", 1),), 2)
    widened = advance(padded, speed, drift, kappa)
    widened = jnp.where(inside, widened, jnp.float32(0.0))
    first = widened[:, 1:-1]
    second = advance(widened, speed, drift, kappa)
    defect = mask[0][None] * (observed[0] - first) + mask[1][None] * (observed[1] - second)
    prior_end = passed_along(second, "win", 1)
    mismatch = jnp.where(win_index > 0, field - prior_end, jnp.float32(0.0))
    lam = lam + 0.5 * mismatch
    carried = prefix(lam, "win", lambda earlier, later: earlier + later, jnp.zeros_like(lam))
    resid = defect + lam - carried / divisor
    spectral = jnp.matmul(resid, h_lon, precision=high)
    spectral = lax.all_to_all(spectral, "lat", split_axis=2, concat_axis=1, tiled=True)
    spectral = jnp.einsum("ij,ljk->lik", h_lat, spectral, precision=high) * weight
    spectral = jnp.einsum("ij,ljk->lik", h_lat, spectral, precision=high)
    spectral = lax.all_to_all(spectral, "lat", split_axis=1, concat_axis=2, tiled=True)
    increment = jnp.matmul(spectral, h_lon, precision=high) / (nlat * nlon)
    field = field + 0.5 * increment
    return (field[None], lam[None])


def split(value):
    hi = value.astype(jnp.bfloat16)
    return hi, (value - hi.astype(jnp.float32)).astype(jnp.bfloat16)


def stencil(scal, field, north, south):
    width = field.shape[1]
    east = pltpu.roll(field, width - 1, 1)
    west = pltpu.roll(field, 1, 1)
    return (
        field
        - scal[0] * field * (east - west) * 0.5
        - scal[1] * (north - south) * 0.5
        + scal[2] * (east + west + north + south - 4.0 * field)
    )


def weight_of(here_ref, table):
    return lambda number: table[here_ref[1], number]


def windowed(weight, x, mult, ended):
    half = x.shape[1] // 2
    sent = weight(SIGN) * ended + weight(SHARE) * (mult + weight(OWN) * x)
    return [part for value in (ended, sent) for part in
            (value[:, :half] + value[:, half:], value[:, :half] - value[:, half:])]


def forecast_kernel(here_ref, table, speed, drift, kappa, x_ref, mult_ref, x1_ref, *outs):
    band = x_ref.shape[0]
    weight, scal = weight_of(here_ref, table), (speed[0], drift[0], kappa[0])

    def step(source, at, count):
        return stencil(scal, source[at:at + count], source[at + 1:at + count + 1], source[at - 1:at + count - 1])

    x1_ref[ROWS - 1:ROWS] = step(x_ref, ROWS - 1, 1)
    x1_ref[band - ROWS:band - ROWS + 1] = step(x_ref, band - ROWS, 1)
    for at in range(ROWS, band - ROWS, ROWS):
        x1_ref[at:at + ROWS] = step(x_ref, at, ROWS)
    for at in range(ROWS, band - ROWS, ROWS):
        rows = slice(at, at + ROWS)
        parts = windowed(weight, x_ref[rows], mult_ref[rows], 0.5 * step(x1_ref, at, ROWS))
        for out, part in zip(outs, parts):
            out[rows] = part


def edge_kernel(bands, here_ref, table, speed, drift, kappa, x_ref, mult_ref, low_ref, high_ref, *refs):
    outs, (ext, mid, whole, parts, sems) = refs[5:10], refs[10:]
    band = x_ref.shape[0]
    edge = low_ref.shape[0]
    weight, scal = weight_of(here_ref, table), (speed[0], drift[0], kappa[0])
    copies = []
    for end in range(2):
        at = 0 if end == 0 else band - ROWS
        if end == 0:
            ext[end, ROWS - edge:ROWS] = low_ref[...]
            ext[end, ROWS:3 * ROWS] = x_ref[:2 * ROWS]
        else:
            ext[end, :2 * ROWS] = x_ref[band - 2 * ROWS:]
            ext[end, 2 * ROWS:2 * ROWS + edge] = high_ref[...]

        def step(source, row, count):
            return stencil(scal, source[end, row:row + count], source[end, row + 1:row + count + 1],
                           source[end, row - 1:row + count - 1])

        before, after = step(ext, ROWS - 1, 1), step(ext, 2 * ROWS, 1)
        if end == 0:
            before = before * jnp.where(here_ref[0] > 0, 1.0, 0.0)
        else:
            after = after * jnp.where(here_ref[0] < bands - 1, 1.0, 0.0)
        mid[end, ROWS - 1:ROWS] = before
        mid[end, 2 * ROWS:2 * ROWS + 1] = after
        mid[end, ROWS:2 * ROWS] = step(ext, ROWS, ROWS)
        rows = slice(at, at + ROWS)
        whole[end] = mid[end, ROWS:2 * ROWS]
        for number, part in enumerate(windowed(weight, x_ref[rows], mult_ref[rows], 0.5 * step(mid, ROWS, ROWS))):
            parts[end, number] = part
        sources = [whole.at[end]] + [parts.at[end, number] for number in range(4)]
        for number, (source, out) in enumerate(zip(sources, outs)):
            copies.append(pltpu.make_async_copy(source, out.at[rows], sems.at[end, number]))
            copies[-1].start()
    for copy in copies:
        copy.wait()


def forecast(here, bands, scal, x, mult, exchange_edges):
    band, width = x.shape
    shapes = [jax.ShapeDtypeStruct((band, width), jnp.float32)]
    shapes += [jax.ShapeDtypeStruct((band, width // 2), jnp.float32)] * 4
    table = jnp.asarray(WEIGHTS)
    inner = pl.pallas_call(
        forecast_kernel,
        out_shape=shapes,
        in_specs=[SMEM] * 5 + [VMEM] * 2,
        out_specs=[VMEM] * 5,
        compiler_params=LIMIT,
        cost_estimate=pl.CostEstimate(flops=40 * band * width, bytes_accessed=20 * band * width, transcendentals=0),
        name="forecast",
    )(here, table, *scal, x, mult)
    low, high = exchange_edges
    return pl.pallas_call(
        functools.partial(edge_kernel, bands),
        out_shape=shapes,
        in_specs=[SMEM] * 5 + [VMEM] * 4 + [ANY] * 5,
        out_specs=[ANY] * 5,
        input_output_aliases={9 + number: number for number in range(5)},
        scratch_shapes=[pltpu.VMEM((2, 4 * ROWS, width), jnp.float32)] * 2 + [
            pltpu.VMEM((2, ROWS, width), jnp.float32),
            pltpu.VMEM((2, 4, ROWS, width // 2), jnp.float32),
            pltpu.SemaphoreType.DMA((2, 5)),
        ],
        compiler_params=LIMIT,
        cost_estimate=pl.CostEstimate(flops=1000 * width, bytes_accessed=400 * width, transcendentals=0),
        name="edges",
    )(here, table, *scal, x, mult, low, high, *inner)


def defect_kernel(here_ref, table, x_ref, mult_ref, obs_ref, mask_ref, x1_ref, plus_ref, minus_ref,
                  base_plus, base_minus, step_plus, second_ref, third_ref):
    half = x_ref.shape[1] // 2
    weight = weight_of(here_ref, table)
    for at in range(0, x_ref.shape[0], ROWS):
        rows = slice(at, at + ROWS)
        plus, minus = plus_ref[rows], minus_ref[rows]
        base, own = [], []
        for cols, end in ((slice(0, half), plus + minus), (slice(half, 2 * half), plus - minus)):
            part = mult_ref[rows, cols] + weight(OWN) * x_ref[rows, cols]
            own.append(part)
            seen = mask_ref[:, rows, cols].astype(jnp.float32)
            base.append(
                part + seen[0] * (obs_ref[0, rows, cols] - x1_ref[rows, cols])
                + seen[1] * (obs_ref[1, rows, cols] - end)
            )
        base_plus[rows] = base[0] + base[1]
        base_minus[rows] = base[0] - base[1]
        own_plus, own_minus = own[0] + own[1], own[0] - own[1]
        step_plus[rows] = own_plus - plus
        second_ref[rows] = jnp.where(weight(FIRST) > 0.0, plus + own_plus * weight(SHARE), minus + own_minus * weight(SHARE))
        third_ref[rows] = jnp.where(weight(FIRST) > 0.0, minus + own_minus * weight(SHARE), own_minus - minus)


def defect(here, x, mult, obs, mask, x1, plus, minus):
    band, width = x.shape
    rows = 4 * ROWS
    whole = pl.BlockSpec((rows, width), lambda i: (i, 0))
    pair = pl.BlockSpec((2, rows, width), lambda i: (0, i, 0))
    part = pl.BlockSpec((rows, width // 2), lambda i: (i, 0))
    return pl.pallas_call(
        defect_kernel,
        grid=(band // rows,),
        out_shape=[jax.ShapeDtypeStruct((band, width // 2), jnp.float32)] * 5,
        in_specs=[SMEM, SMEM, whole, whole, pair, pair, whole, part, part],
        out_specs=[part] * 5,
        compiler_params=LIMIT,
        cost_estimate=pl.CostEstimate(flops=30 * band * width, bytes_accessed=40 * band * width, transcendentals=0),
        name="defect",
    )(here, jnp.asarray(WEIGHTS), x, mult, obs, mask, x1, plus, minus)


def resid_kernel(bands, first, here_ref, table, base_ref, *refs):
    weight = weight_of(here_ref, table)
    terms, outs = refs[:-bands], refs[-bands:]
    columns = outs[0].shape[1]
    for shift in range(bands):
        target = lax.rem(here_ref[0] + shift, bands)
        at = pl.ds(pl.multiple_of(target * columns, columns), columns)
        value = base_ref[:, at]
        for number, term in enumerate(terms):
            value = value - weight(first + number) * term[:, at]
        outs[shift][...] = value


def resid_blocks(here, bands, first, base, terms):
    band, half = base.shape
    columns = half // bands
    return pl.pallas_call(
        functools.partial(resid_kernel, bands, first),
        out_shape=[jax.ShapeDtypeStruct((band, columns), jnp.float32)] * bands,
        in_specs=[SMEM, SMEM] + [VMEM] * (1 + len(terms)),
        out_specs=[VMEM] * bands,
        compiler_params=LIMIT,
        cost_estimate=pl.CostEstimate(flops=8 * band * half, bytes_accessed=24 * band * half, transcendentals=0),
        name="resid_blocks",
    )(here, jnp.asarray(WEIGHTS), base, *terms)


def lat_kernel(bands, here_ref, *refs):
    blocks, (ehi, elo, ohi, olo) = refs[:bands], refs[bands:bands + 4]
    outs, (gathered, mixed) = refs[bands + 4:2 * bands + 4], refs[2 * bands + 4:]
    here = here_ref[0]
    pairs = bands // 2
    band, columns = blocks[0].shape
    for shift in range(pairs):
        source = lax.rem(here - shift + bands, bands)
        rows = pl.ds(pl.multiple_of(lax.rem(source, pairs) * band, band), band)
        first, other = blocks[shift][...], blocks[shift + pairs][...]
        sign = jnp.where(source < pairs, 1.0, -1.0)
        for part, value in enumerate((first + other, (first - other) * sign)):
            hi, lo = split(value)
            gathered[part, rows, :columns] = hi
            gathered[part, rows, columns:] = lo
    dot = functools.partial(jnp.dot, preferred_element_type=jnp.float32)
    for part, (hi, lo) in enumerate(((ehi, elo), (ohi, olo))):
        both = dot(hi[...], gathered[part])
        mixed[part] = both[:, :columns] + both[:, columns:] + dot(lo[...], gathered[part, :, :columns])
    for shift in range(bands):
        target = lax.rem(here + shift, bands)
        rows = pl.ds(pl.multiple_of(lax.rem(target, pairs) * band, band), band)
        sign = jnp.where(target < pairs, 1.0, -1.0)
        outs[shift][...] = mixed[0, rows] + sign * mixed[1, rows]


def lat_apply(here, blocks, matrices):
    bands = len(blocks)
    band, columns = blocks[0].shape
    half = matrices[0].shape[0]
    return pl.pallas_call(
        functools.partial(lat_kernel, bands),
        out_shape=[jax.ShapeDtypeStruct((band, columns), jnp.float32)] * bands,
        in_specs=[SMEM] + [VMEM] * (bands + 4),
        out_specs=[VMEM] * bands,
        scratch_shapes=[
            pltpu.VMEM((2, half, 2 * columns), jnp.bfloat16),
            pltpu.VMEM((2, half, columns), jnp.float32),
        ],
        compiler_params=LIMIT,
        cost_estimate=pl.CostEstimate(
            flops=12 * half * half * columns, bytes_accessed=8 * half * half, transcendentals=0
        ),
        name="lat_apply",
    )(here, *blocks, *matrices)


def gather_rows(here, bands, blocks, gathered):
    band, columns = blocks[0].shape
    for shift in range(bands):
        source = lax.rem(here - shift + bands, bands)
        at = pl.ds(pl.multiple_of(source * columns, columns), columns)
        hi, lo = split(blocks[shift][...])
        gathered[:band, at] = hi
        gathered[band:, at] = lo


def lon_product(band, hi, lo, gathered):
    dot = functools.partial(jnp.dot, preferred_element_type=jnp.float32)
    both = dot(gathered[...], hi[...])
    return both[:band] + both[band:] + dot(gathered[:band], lo[...])


def lon_even_kernel(bands, here_ref, *refs):
    blocks, (hi, lo, out, gathered) = refs[:bands], refs[bands:]
    gather_rows(here_ref[0], bands, blocks, gathered)
    out[...] = lon_product(blocks[0].shape[0], hi, lo, gathered)


def lon_odd_kernel(bands, here_ref, *refs):
    blocks, (hi, lo, even, field, out, gathered) = refs[:bands], refs[bands:]
    gather_rows(here_ref[0], bands, blocks, gathered)
    half = hi.shape[0]
    odd = lon_product(blocks[0].shape[0], hi, lo, gathered)
    out[:, :half] = field[:, :half] + 0.5 * (even[...] + odd)
    out[:, half:] = field[:, half:] + 0.5 * (even[...] - odd)


def lon_apply(here, blocks, matrices, extra=()):
    bands = len(blocks)
    band, _ = blocks[0].shape
    half = matrices[0].shape[0]
    return pl.pallas_call(
        functools.partial(lon_odd_kernel if extra else lon_even_kernel, bands),
        out_shape=jax.ShapeDtypeStruct((band, 2 * half if extra else half), jnp.float32),
        in_specs=[SMEM] + [VMEM] * (bands + 2 + len(extra)),
        out_specs=VMEM,
        scratch_shapes=[pltpu.VMEM((2 * band, half), jnp.bfloat16)],
        compiler_params=LIMIT,
        cost_estimate=pl.CostEstimate(
            flops=6 * band * half * half, bytes_accessed=4 * half * half, transcendentals=0
        ),
        name="lon_apply",
    )(here, *blocks, *matrices, *extra)


def mix_kernel(here_ref, table, near_ref, side_ref, step_ref, second_ref, far_ref, cross_ref):
    weight = weight_of(here_ref, table)
    for at in range(0, near_ref.shape[0], ROWS):
        rows = slice(at, at + ROWS)
        far_ref[rows] = near_ref[rows] + weight(ONWARD) * step_ref[rows]
        cross_ref[rows] = weight(SECOND) * second_ref[rows] + weight(SIDE) * side_ref[rows]


def mix(here, near, side, step_plus, second):
    shape = jax.ShapeDtypeStruct(near.shape, jnp.float32)
    return pl.pallas_call(
        mix_kernel,
        out_shape=[shape] * 2,
        in_specs=[SMEM] * 2 + [VMEM] * 4,
        out_specs=[VMEM] * 2,
        compiler_params=LIMIT,
        cost_estimate=pl.CostEstimate(flops=5 * near.size, bytes_accessed=24 * near.size, transcendentals=0),
        name="mix",
    )(here, jnp.asarray(WEIGHTS), near, side, step_plus, second)


def multiplier_kernel(here_ref, table, x_ref, mult_ref, plus_ref, minus_ref, near_ref, cross_ref, out_ref):
    weight = weight_of(here_ref, table)
    half = x_ref.shape[1] // 2
    known = weight(KNOWN)
    for at in range(0, x_ref.shape[0], ROWS):
        rows = slice(at, at + ROWS)
        plus = plus_ref[rows] + known * (cross_ref[rows] - near_ref[rows])
        minus = minus_ref[rows]
        for cols, end in ((slice(0, half), plus + minus), (slice(half, 2 * half), plus - minus)):
            out_ref[rows, cols] = mult_ref[rows, cols] + weight(OWN) * x_ref[rows, cols] - 0.5 * end


def new_multipliers(here, x, mult, plus, minus, near, cross):
    band, width = x.shape
    rows = 4 * ROWS
    whole = pl.BlockSpec((rows, width), lambda i: (i, 0))
    part = pl.BlockSpec((rows, width // 2), lambda i: (i, 0))
    return pl.pallas_call(
        multiplier_kernel,
        grid=(band // rows,),
        out_shape=jax.ShapeDtypeStruct((band, width), jnp.float32),
        in_specs=[SMEM] * 2 + [whole] * 2 + [part] * 4,
        out_specs=whole,
        compiler_params=LIMIT,
        cost_estimate=pl.CostEstimate(flops=6 * band * width, bytes_accessed=20 * band * width, transcendentals=0),
        name="new_multipliers",
    )(here, jnp.asarray(WEIGHTS), x, mult, plus, minus, near, cross)


def exchange(blocks):
    bands = len(blocks)
    moved = [blocks[0]]
    for shift in range(1, bands):
        route = [(source, (source + shift) % bands) for source in range(bands)]
        moved.append(lax.ppermute(blocks[shift], "lat", route))
    return moved


WEIGHTS = np.array([
    [0.0, 1.0, -1.0, 1.0, 0.5, 1.0, 0.0, 0.0, 0.0, 0.0, 0.0, 0.0, 0.0, 0.0],
    [0.5, 1 / 2, 1.0, 0.0, 1.0, 0.0, 0.0, 0.0, 0.0, 1.0, 0.0, 0.0, 1.0, 0.5],
    [0.5, 1 / 3, 1.0, 0.0, 0.0, 1.0, 1 / 3, 0.0, 1.0, 0.0, 0.5, 1.0, 0.0, 0.0],
    [0.5, 1 / 4, 1.0, 0.0, 0.0, 0.0, 1.0, 1.0, 1 / 3, 0.0, 0.0, 1.0, 1 / 3, 0.0],
], np.float32)
OWN, SHARE, SIGN, FIRST, ONWARD, SECOND, SIDE, EVEN, ODD, KNOWN = 0, 1, 2, 3, 4, 5, 6, 7, 10, 13


def per_device(
    state, multipliers, observations, obs_mask, speed, drift, kappa, lat_spectrum, lon_spectrum
):
    bands, windows = lax.axis_size("lat"), lax.axis_size("win")
    band, nlon = state.shape[2:]
    columns = nlon // 2 // bands
    if windows != 4 or state.shape[1] != 1 or bands % 2 or band % LANES or columns % LANES:
        return per_device_any(
            state, multipliers, observations, obs_mask, speed, drift, kappa, lat_spectrum, lon_spectrum
        )
    return per_device_hops(
        state, multipliers, observations, obs_mask, speed, drift, kappa, lat_spectrum, lon_spectrum
    )


def per_device_hops(
    state, multipliers, observations, obs_mask, speed, drift, kappa, lat_spectrum, lon_spectrum
):
    bands = lax.axis_size("lat")
    here = jnp.stack([lax.axis_index("lat"), lax.axis_index("win")]).astype(jnp.int32)
    x, mult = state[0, 0], multipliers[0, 0]
    edges = (
        lax.ppermute(x[-2:], "lat", [(i, i + 1) for i in range(bands - 1)]),
        lax.ppermute(x[:2], "lat", [(i + 1, i) for i in range(bands - 1)]),
    )
    x1, plus, minus, near, side = forecast(here, bands, (speed, drift, kappa), x, mult, edges)
    near = lax.ppermute(near, "win", [(0, 1), (1, 0), (2, 3)])
    side = lax.ppermute(side, "win", [(0, 2), (1, 3)])
    base_plus, base_minus, step_plus, second, third = defect(
        here, x, mult, observations[0, :, 0], obs_mask[0], x1, plus, minus
    )
    lat_matrices, step_plus, second = lax.optimization_barrier((build(lat_spectrum), step_plus, second))
    far, cross = mix(here, near, side, step_plus, second)
    far = lax.ppermute(far, "win", [(0, 2), (1, 3)])
    cross = lax.ppermute(cross, "win", [(0, 1), (2, 3), (3, 2)])
    even = list(resid_blocks(here, bands, EVEN, base_plus, (near, far, cross)))
    lon_matrices, third, even[0] = lax.optimization_barrier((build(lon_spectrum), third, even[0]))
    third = lax.ppermute(third, "win", [(0, 1), (1, 3)])
    odd = resid_blocks(here, bands, ODD, base_minus, (side, cross, third))
    plus = lax.ppermute(plus, "win", [(1, 2), (2, 3)])
    minus = lax.ppermute(minus, "win", [(0, 1), (1, 2), (2, 3)])
    even, odd = exchange(even), exchange(odd)
    even = exchange(lat_apply(here, even, lat_matrices))
    odd = exchange(lat_apply(here, odd, lat_matrices))
    even = lon_apply(here, even, lon_matrices[:2])
    field = lon_apply(here, odd, lon_matrices[2:], (even, x))
    lam = new_multipliers(here, x, mult, plus, minus, near, cross)
    return (field[None, None], lam[None, None])


def solution(mesh):
    return jax.shard_map(
        per_device,
        mesh=mesh,
        in_specs=(
            P("win", None, "lat", None),
            P("win", None, "lat", None),
            P("win", None, None, "lat", None),
            P("win", None, "lat", None),
            P(),
            P(),
            P(),
            P(),
            P(),
        ),
        out_specs=(P("win", None, "lat", None), P("win", None, "lat", None)),
        check_vma=False,
    )
```

```python
import functools
import math

import numpy as np
import jax
import jax.numpy as jnp
from jax import lax
from jax.experimental import pallas as pl
from jax.experimental.pallas import tpu as pltpu
from jax.sharding import PartitionSpec as P


LANES = 128
ROWS = 8
WEIGHTS = (
    (0.0, 1.0, -1.0, 1.0, 0.5, 1.0, 0.0, 0.0, 0.0, 0.0, 0.0, 0.0, 0.0, 0.0),
    (0.5, 1 / 2, 1.0, 0.0, 1.0, 0.0, 0.0, 0.0, 0.0, 1.0, 0.0, 0.0, 1.0, 0.5),
    (0.5, 1 / 3, 1.0, 0.0, 0.0, 1.0, 1 / 3, 0.0, 1.0, 0.0, 0.5, 1.0, 0.0, 0.0),
    (0.5, 1 / 4, 1.0, 0.0, 0.0, 0.0, 1.0, 1.0, 1 / 3, 0.0, 0.0, 1.0, 1 / 3, 0.0),
)
OWN, SHARE, SIGN, FIRST, ONWARD, SECOND, SIDE, EVEN, ODD, KNOWN = 0, 1, 2, 3, 4, 5, 6, 7, 10, 13
VMEM = pl.BlockSpec(memory_space=pltpu.VMEM)
SMEM = pl.BlockSpec(memory_space=pltpu.SMEM)
ANY = pl.BlockSpec(memory_space=pl.ANY)
HBM = pl.BlockSpec(memory_space=pltpu.HBM)
LIMIT = pltpu.CompilerParams(vmem_limit_bytes=16 * 2**20)


def trig_tables(count):
    low = count // LANES
    blocks = low // 2
    turn = 2.0 * math.pi
    fine = np.arange(LANES)
    coarse = np.arange(low)
    inner = turn * ((coarse[:, None] * fine[None, :]) % low) / low
    middle = turn * (((fine // low)[:, None] * fine[None, :]) % LANES) / LANES
    member = (coarse[:, None] == (fine % low)[None, :]).astype(np.float32)
    twist = turn * (coarse[:, None] * fine[None, :]) / count
    outer = turn * ((np.arange(blocks)[:, None] * coarse[None, :]) % low) / low
    even = (coarse % 2 == 0)[None, :]
    keep = np.concatenate([np.broadcast_to(even, outer.shape), np.broadcast_to(~even, outer.shape)])
    outer = np.concatenate([outer, outer])
    pack = lambda angle, scale: np.concatenate([np.cos(angle), np.sin(angle)], axis=1) * scale
    return (pack(inner, 1.0).astype(np.float32), pack(middle, 1.0).astype(np.float32), member, pack(twist, 1.0 / count).astype(np.float32),
            (np.cos(outer) * keep).astype(np.float32), (np.sin(outer) * keep).astype(np.float32))


def build_kernel(count, d_ref, inner_ref, middle_ref, member_ref, twist_ref, cos_ref, sin_ref, even_hi, even_lo, odd_hi, odd_lo, toep, hank):
    blocks = count // LANES // 2
    high = lax.Precision.HIGHEST
    mm = functools.partial(jnp.dot, precision=high, preferred_element_type=jnp.float32)

    def turned(value, table):
        real, imag = value[:, :LANES], value[:, LANES:]
        tc, ts = table[:, :LANES], table[:, LANES:]
        return jnp.concatenate([real * tc - imag * ts, real * ts + imag * tc], axis=1)

    spectrum = jnp.concatenate([d_ref[:, at:at + LANES] for at in range(0, count, LANES)], axis=0)
    g = lax.dot_general(spectrum, inner_ref[...], (((0,), (0,)), ((), ())), precision=high,
                        preferred_element_type=jnp.float32)
    g = turned(mm(member_ref[...], turned(g, middle_ref)), twist_ref)
    gc, gs = g[:, :LANES], g[:, LANES:]
    c = mm(cos_ref[...], gc) - mm(sin_ref[...], gs)
    s = mm(sin_ref[...], gc) + mm(cos_ref[...], gs)
    rows = lax.broadcasted_iota(jnp.int32, (LANES, LANES), 0)
    cols = lax.broadcasted_iota(jnp.int32, (LANES, LANES), 1)
    flip = jnp.where(rows + cols == LANES - 1, 1.0, 0.0)
    for part in range(2):
        wrap = 1.0 if part == 0 else -1.0
        hi_ref, lo_ref = (even_hi, even_lo) if part == 0 else (odd_hi, odd_lo)

        def row(table, at):
            sign = 1.0
            if at < 0 or at >= blocks:
                sign, at = wrap, at % blocks
            at += part * blocks
            return sign * table[at:at + 1]

        for b in range(blocks):
            window = jnp.concatenate([row(c, b - 1), row(c, b)], axis=1)
            window = jnp.broadcast_to(window, (LANES, 2 * LANES))
            toep[b] = pltpu.roll(window, 0, 1, stride=1, stride_axis=0)[:, LANES:]
            window = jnp.concatenate([row(s, b), row(s, b + 1)], axis=1)
            window = jnp.broadcast_to(window, (LANES, 2 * LANES))
            window = pltpu.roll(window, LANES + 1, 1, stride=1, stride_axis=0)[:, :LANES]
            hank[b] = mm(flip, window)

        def body(i, _):
            for j in range(blocks):
                t = toep[lax.rem(j - i + blocks, blocks)]
                h = hank[lax.rem(i + j, blocks)]
                if part == 1:
                    t = t * jnp.where(j < i, -1.0, 1.0)
                    h = h * jnp.where(i + j >= blocks, -1.0, 1.0)
                a = t + h
                hi = a.astype(jnp.bfloat16)
                at = (pl.ds(pl.multiple_of(i * LANES, LANES), LANES), pl.ds(j * LANES, LANES))
                hi_ref[at] = hi
                lo_ref[at] = (a - hi.astype(jnp.float32)).astype(jnp.bfloat16)
            return 0

        lax.fori_loop(0, blocks, body, 0)


def build(spectrum):
    count = spectrum.shape[1]
    half = count // 2
    tables = trig_tables(count)
    shape = jax.ShapeDtypeStruct((half, half), jnp.bfloat16)
    return pl.pallas_call(
        functools.partial(build_kernel, count),
        out_shape=[shape] * 4, in_specs=[VMEM] * 7, out_specs=[VMEM] * 4,
        scratch_shapes=[pltpu.VMEM((half // LANES, LANES, LANES), jnp.float32)] * 2,
        compiler_params=LIMIT,
        cost_estimate=pl.CostEstimate(flops=2 * half * half * 8, bytes_accessed=8 * half * half, transcendentals=0),
    )(spectrum, *tables)


def extended(block, sides, width):
    for axis, dim in sides:
        count = lax.axis_size(axis)
        forward = [(i, i + 1) for i in range(count - 1)]
        backward = [(target, source) for source, target in forward]
        low = lax.ppermute(
            lax.slice_in_dim(block, block.shape[dim] - width, None, axis=dim), axis, forward
        )
        high = lax.ppermute(lax.slice_in_dim(block, 0, width, axis=dim), axis, backward)
        block = jnp.concatenate([low, block, high], axis=dim)
    return block


def passed_along(value, axis, steps):
    count = lax.axis_size(axis)
    first, last = (max(0, -steps), min(count, count - steps))
    return lax.ppermute(value, axis, [(source, source + steps) for source in range(first, last)])


def prefix(array, axis, combine, identity):
    peers, here = (lax.axis_size(axis), lax.axis_index(axis))
    everything = lax.all_gather(array, axis)
    start = jnp.broadcast_to(jnp.asarray(identity, array.dtype), array.shape)

    def turn(k, before):
        reached = k < here
        new = combine(before, everything[k])
        return jnp.where(reached, new, before)

    return lax.fori_loop(0, peers, turn, start)


def hartley(count):
    index = jnp.arange(count, dtype=jnp.int32)
    product = index[:, None] * index[None, :] % count
    angle = product.astype(jnp.float32) * (2.0 * math.pi / count)
    return jnp.cos(angle) + jnp.sin(angle)


def advance(padded, speed, drift, kappa):
    field = padded[:, 1:-1]
    north = padded[:, 2:]
    south = padded[:, :-2]
    east = jnp.roll(field, -1, axis=-1)
    west = jnp.roll(field, 1, axis=-1)
    speed_c = speed[:, None, None]
    drift_c = drift[:, None, None]
    kappa_c = kappa[:, None, None]
    return (
        field
        - speed_c * field * (east - west) * 0.5
        - drift_c * (north - south) * 0.5
        + kappa_c * (east + west + north + south - 4.0 * field)
    )


def per_device_any(
    state, multipliers, observations, obs_mask, speed, drift, kappa, lat_spectrum, lon_spectrum
):
    high = lax.Precision.HIGHEST
    field = state[0]
    lam = multipliers[0]
    observed = observations[0]
    mask = obs_mask[0].astype(jnp.float32)
    band = field.shape[1]
    nlon = field.shape[2]
    bands = lax.axis_size("lat")
    nlat = band * bands
    columns = nlon // bands
    lat_index = lax.axis_index("lat")
    win_index = lax.axis_index("win")
    h_lon = hartley(nlon)
    h_lat = hartley(nlat)
    lon_part = lax.dynamic_slice_in_dim(lon_spectrum, lat_index * columns, columns, 1)
    weight = lat_spectrum[:, :, None] * lon_part[:, None, :]
    divisor = jnp.maximum(win_index, 1).astype(jnp.float32)
    rows_global = lat_index * band + jnp.arange(-1, band + 1, dtype=jnp.int32)
    inside = ((rows_global >= 0) & (rows_global < nlat))[None, :, None]
    padded = extended(field, (("lat", 1),), 2)
    widened = advance(padded, speed, drift, kappa)
    widened = jnp.where(inside, widened, jnp.float32(0.0))
    first = widened[:, 1:-1]
    second = advance(widened, speed, drift, kappa)
    defect = mask[0][None] * (observed[0] - first) + mask[1][None] * (observed[1] - second)
    prior_end = passed_along(second, "win", 1)
    mismatch = jnp.where(win_index > 0, field - prior_end, jnp.float32(0.0))
    lam = lam + 0.5 * mismatch
    carried = prefix(lam, "win", lambda earlier, later: earlier + later, jnp.zeros_like(lam))
    resid = defect + lam - carried / divisor
    spectral = jnp.matmul(resid, h_lon, precision=high)
    spectral = lax.all_to_all(spectral, "lat", split_axis=2, concat_axis=1, tiled=True)
    spectral = jnp.einsum("ij,ljk->lik", h_lat, spectral, precision=high) * weight
    spectral = jnp.einsum("ij,ljk->lik", h_lat, spectral, precision=high)
    spectral = lax.all_to_all(spectral, "lat", split_axis=1, concat_axis=2, tiled=True)
    increment = jnp.matmul(spectral, h_lon, precision=high) / (nlat * nlon)
    field = field + 0.5 * increment
    return (field[None], lam[None])


def split(value):
    hi = value.astype(jnp.bfloat16)
    return hi, (value - hi.astype(jnp.float32)).astype(jnp.bfloat16)


def stencil(scal, field, north, south):
    width = field.shape[1]
    east = pltpu.roll(field, width - 1, 1)
    west = pltpu.roll(field, 1, 1)
    return (
        field
        - scal[0] * field * (east - west) * 0.5
        - scal[1] * (north - south) * 0.5
        + scal[2] * (east + west + north + south - 4.0 * field)
    )


def weight_of(here_ref):
    def pick(number):
        value = WEIGHTS[0][number]
        for window in range(1, len(WEIGHTS)):
            value = jnp.where(here_ref[1] == window, WEIGHTS[window][number], value)
        return value

    return pick


def windowed(weight, own, ended):
    half = own.shape[1] // 2
    values = (ended, weight(SIGN) * ended + weight(SHARE) * own)
    return [part for value in values for part in
            (value[:, :half] + value[:, half:], value[:, :half] - value[:, half:])]


def forecast_kernel(here_ref, speed, drift, kappa, x_hbm, mult_hbm, x_ref, own_ref, x1_ref, *refs):
    outs, (mult_ref, sems) = refs[:4], refs[4:]
    band = x_ref.shape[0]
    chunk = band // 4
    weight, scal = weight_of(here_ref), (speed[0], drift[0], kappa[0])

    def step(source, at, count):
        return stencil(scal, source[at:at + count], source[at + 1:at + count + 1], source[at - 1:at + count - 1])

    copies = []
    for number, (source, target) in enumerate(((x_hbm, x_ref), (mult_hbm, mult_ref))):
        for part in range(4):
            rows = slice(part * chunk, (part + 1) * chunk)
            copies.append(pltpu.make_async_copy(source.at[rows], target.at[rows], sems.at[number, part]))
            copies[-1].start()
    ready, stepped = 0, ROWS
    for part in range(4):
        copies[part].wait()
        ready += chunk
        if part == 0:
            x1_ref[ROWS - 1:ROWS] = step(x_ref, ROWS - 1, 1)
        while stepped + ROWS < ready:
            x1_ref[stepped:stepped + ROWS] = step(x_ref, stepped, ROWS)
            stepped += ROWS
    x1_ref[stepped:stepped + 1] = step(x_ref, stepped, 1)
    for part in range(4):
        copies[4 + part].wait()
        for at in range(part * chunk, (part + 1) * chunk, ROWS):
            rows = slice(at, at + ROWS)
            own = mult_ref[rows] + weight(OWN) * x_ref[rows]
            own_ref[rows] = own
            if 0 < at < band - ROWS:
                for out, value in zip(outs, windowed(weight, own, 0.5 * step(x1_ref, at, ROWS))):
                    out[rows] = value


def edge_kernel(bands, here_ref, speed, drift, kappa, x_ref, own_ref, low_ref, high_ref, *refs):
    outs, (ext, mid, whole, parts, sems) = refs[5:10], refs[10:]
    band = x_ref.shape[0]
    edge = low_ref.shape[0]
    weight, scal = weight_of(here_ref), (speed[0], drift[0], kappa[0])
    copies = []
    for end in range(2):
        at = 0 if end == 0 else band - ROWS
        if end == 0:
            ext[end, ROWS - edge:ROWS] = low_ref[...]
            ext[end, ROWS:3 * ROWS] = x_ref[:2 * ROWS]
        else:
            ext[end, :2 * ROWS] = x_ref[band - 2 * ROWS:]
            ext[end, 2 * ROWS:2 * ROWS + edge] = high_ref[...]

        def step(source, row, count):
            return stencil(scal, source[end, row:row + count], source[end, row + 1:row + count + 1],
                           source[end, row - 1:row + count - 1])

        before, after = step(ext, ROWS - 1, 1), step(ext, 2 * ROWS, 1)
        if end == 0:
            before = before * jnp.where(here_ref[0] > 0, 1.0, 0.0)
        else:
            after = after * jnp.where(here_ref[0] < bands - 1, 1.0, 0.0)
        mid[end, ROWS - 1:ROWS] = before
        mid[end, 2 * ROWS:2 * ROWS + 1] = after
        mid[end, ROWS:2 * ROWS] = step(ext, ROWS, ROWS)
        rows = slice(at, at + ROWS)
        whole[end] = mid[end, ROWS:2 * ROWS]
        for number, part in enumerate(windowed(weight, own_ref[rows], 0.5 * step(mid, ROWS, ROWS))):
            parts[end, number] = part
        sources = [whole.at[end]] + [parts.at[end, number] for number in range(4)]
        for number, (source, out) in enumerate(zip(sources, outs)):
            copies.append(pltpu.make_async_copy(source, out.at[rows], sems.at[end, number]))
            copies[-1].start()
    for copy in copies:
        copy.wait()


def forecast(here, bands, scal, x, mult, exchange_edges):
    band, width = x.shape
    whole = jax.ShapeDtypeStruct((band, width), jnp.float32)
    shapes = [whole] + [jax.ShapeDtypeStruct((band, width // 2), jnp.float32)] * 4
    x, own, *inner = pl.pallas_call(
        forecast_kernel,
        out_shape=[whole] * 2 + shapes,
        in_specs=[SMEM] * 4 + [HBM] * 2,
        out_specs=[VMEM] * 7,
        scratch_shapes=[pltpu.VMEM((band, width), jnp.float32), pltpu.SemaphoreType.DMA((2, 4))],
        compiler_params=LIMIT,
        cost_estimate=pl.CostEstimate(flops=40 * band * width, bytes_accessed=20 * band * width, transcendentals=0),
        name="forecast",
    )(here, *scal, pltpu.with_memory_space_constraint(x, pltpu.HBM), pltpu.with_memory_space_constraint(mult, pltpu.HBM))
    low, high = exchange_edges
    outs = pl.pallas_call(
        functools.partial(edge_kernel, bands),
        out_shape=shapes,
        in_specs=[SMEM] * 4 + [VMEM] * 4 + [ANY] * 5,
        out_specs=[ANY] * 5,
        input_output_aliases={8 + number: number for number in range(5)},
        scratch_shapes=[pltpu.VMEM((2, 4 * ROWS, width), jnp.float32)] * 2 + [
            pltpu.VMEM((2, ROWS, width), jnp.float32),
            pltpu.VMEM((2, 4, ROWS, width // 2), jnp.float32),
            pltpu.SemaphoreType.DMA((2, 5)),
        ],
        compiler_params=LIMIT,
        cost_estimate=pl.CostEstimate(flops=1000 * width, bytes_accessed=400 * width, transcendentals=0),
        name="edges",
    )(here, *scal, x, own, low, high, *inner)
    return x, own, *outs


def defect_kernel(here_ref, own_ref, obs_ref, mask_ref, x1_ref, plus_ref, minus_ref,
                  base_plus, base_minus, step_plus, second_ref, third_ref):
    half = own_ref.shape[1] // 2
    weight = weight_of(here_ref)
    for at in range(0, own_ref.shape[0], ROWS):
        rows = slice(at, at + ROWS)
        plus, minus = plus_ref[rows], minus_ref[rows]
        base, own = [], []
        for cols, end in ((slice(0, half), plus + minus), (slice(half, 2 * half), plus - minus)):
            own.append(own_ref[rows, cols])
            seen = mask_ref[:, rows, cols].astype(jnp.float32)
            base.append(
                own[-1] + seen[0] * (obs_ref[0, rows, cols] - x1_ref[rows, cols])
                + seen[1] * (obs_ref[1, rows, cols] - end)
            )
        base_plus[rows] = base[0] + base[1]
        base_minus[rows] = base[0] - base[1]
        own_plus, own_minus = own[0] + own[1], own[0] - own[1]
        step_plus[rows] = own_plus - plus
        first = weight(FIRST) > 0.0
        sent_minus = minus + weight(SHARE) * own_minus
        second_ref[rows] = jnp.where(first, plus + weight(SHARE) * own_plus, sent_minus)
        third_ref[rows] = jnp.where(first, sent_minus, own_minus - minus)


def defect(here, own, obs, mask, x1, plus, minus):
    band, width = own.shape
    rows = 4 * ROWS
    whole = pl.BlockSpec((rows, width), lambda i: (i, 0))
    pair = pl.BlockSpec((2, rows, width), lambda i: (0, i, 0))
    part = pl.BlockSpec((rows, width // 2), lambda i: (i, 0))
    return pl.pallas_call(
        defect_kernel,
        grid=(band // rows,),
        out_shape=[jax.ShapeDtypeStruct((band, width // 2), jnp.float32)] * 5,
        in_specs=[SMEM, whole, pair, pair, whole, part, part],
        out_specs=[part] * 5,
        compiler_params=LIMIT,
        cost_estimate=pl.CostEstimate(flops=30 * band * width, bytes_accessed=40 * band * width, transcendentals=0),
        name="defect",
    )(here, own, obs, mask, x1, plus, minus)


def mix_kernel(first, here_ref, one_ref, other_ref, out_ref):
    weight = weight_of(here_ref)
    one = one_ref[...] if first is None else weight(first) * one_ref[...]
    out_ref[...] = one + weight(ONWARD if first is None else SIDE) * other_ref[...]


def mix(here, first, one, other):
    return pl.pallas_call(
        functools.partial(mix_kernel, first),
        out_shape=jax.ShapeDtypeStruct(one.shape, jnp.float32),
        in_specs=[SMEM] + [VMEM] * 2,
        out_specs=VMEM,
        compiler_params=LIMIT,
        cost_estimate=pl.CostEstimate(flops=3 * one.size, bytes_accessed=12 * one.size, transcendentals=0),
        name="mix",
    )(here, one, other)


def resid_kernel(bands, first, here_ref, base_ref, *refs):
    terms, outs = refs[:-bands], refs[-bands:]
    weight = weight_of(here_ref)
    columns = outs[0].shape[1]
    for shift in range(bands):
        target = lax.rem(here_ref[0] + shift, bands)
        at = pl.ds(pl.multiple_of(target * columns, columns), columns)
        value = base_ref[:, at]
        for number, term in enumerate(terms):
            value = value - weight(first + number) * term[:, at]
        outs[shift][...] = value


def resid_blocks(here, bands, first, base, *terms):
    band, half = base.shape
    columns = half // bands
    return pl.pallas_call(
        functools.partial(resid_kernel, bands, first),
        out_shape=[jax.ShapeDtypeStruct((band, columns), jnp.float32)] * bands,
        in_specs=[SMEM] + [VMEM] * 4,
        out_specs=[VMEM] * bands,
        compiler_params=LIMIT,
        cost_estimate=pl.CostEstimate(flops=8 * band * half, bytes_accessed=24 * band * half, transcendentals=0),
        name="resid_blocks",
    )(here, base, *terms)


def lat_kernel(bands, here_ref, *refs):
    blocks, (ehi, elo, ohi, olo) = refs[:bands], refs[bands:bands + 4]
    outs, (gathered, mixed) = refs[bands + 4:2 * bands + 4], refs[2 * bands + 4:]
    here = here_ref[0]
    pairs = bands // 2
    band, columns = blocks[0].shape
    for shift in range(pairs):
        source = lax.rem(here - shift + bands, bands)
        rows = pl.ds(pl.multiple_of(lax.rem(source, pairs) * band, band), band)
        first, other = blocks[shift][...], blocks[shift + pairs][...]
        sign = jnp.where(source < pairs, 1.0, -1.0)
        for part, value in enumerate((first + other, (first - other) * sign)):
            hi, lo = split(value)
            gathered[part, rows, :columns] = hi
            gathered[part, rows, columns:] = lo
    dot = functools.partial(jnp.dot, preferred_element_type=jnp.float32)
    for part, (hi, lo) in enumerate(((ehi, elo), (ohi, olo))):
        both = dot(hi[...], gathered[part])
        mixed[part] = both[:, :columns] + both[:, columns:] + dot(lo[...], gathered[part, :, :columns])
    for shift in range(bands):
        target = lax.rem(here + shift, bands)
        rows = pl.ds(pl.multiple_of(lax.rem(target, pairs) * band, band), band)
        sign = jnp.where(target < pairs, 1.0, -1.0)
        outs[shift][...] = mixed[0, rows] + sign * mixed[1, rows]


def lat_apply(here, blocks, matrices):
    bands = len(blocks)
    band, columns = blocks[0].shape
    half = matrices[0].shape[0]
    return pl.pallas_call(
        functools.partial(lat_kernel, bands),
        out_shape=[jax.ShapeDtypeStruct((band, columns), jnp.float32)] * bands,
        in_specs=[SMEM] + [VMEM] * (bands + 4),
        out_specs=[VMEM] * bands,
        scratch_shapes=[
            pltpu.VMEM((2, half, 2 * columns), jnp.bfloat16),
            pltpu.VMEM((2, half, columns), jnp.float32),
        ],
        compiler_params=LIMIT,
        cost_estimate=pl.CostEstimate(
            flops=12 * half * half * columns, bytes_accessed=8 * half * half, transcendentals=0
        ),
        name="lat_apply",
    )(here, *blocks, *matrices)


def gather_rows(here, bands, blocks, gathered):
    band, columns = blocks[0].shape
    for shift in range(bands):
        source = lax.rem(here - shift + bands, bands)
        at = pl.ds(pl.multiple_of(source * columns, columns), columns)
        hi, lo = split(blocks[shift][...])
        gathered[:band, at] = hi
        gathered[band:, at] = lo


def lon_product(band, hi, lo, gathered):
    dot = functools.partial(jnp.dot, preferred_element_type=jnp.float32)
    both = dot(gathered[...], hi[...])
    return both[:band] + both[band:] + dot(gathered[:band], lo[...])


def lon_even_kernel(bands, here_ref, *refs):
    blocks, (hi, lo, out, gathered) = refs[:bands], refs[bands:]
    gather_rows(here_ref[0], bands, blocks, gathered)
    out[...] = lon_product(blocks[0].shape[0], hi, lo, gathered)


def lon_odd_kernel(bands, here_ref, *refs):
    blocks, (hi, lo, even, field, out, gathered) = refs[:bands], refs[bands:]
    gather_rows(here_ref[0], bands, blocks, gathered)
    half = hi.shape[0]
    odd = lon_product(blocks[0].shape[0], hi, lo, gathered)
    out[:, :half] = field[:, :half] + 0.5 * (even[...] + odd)
    out[:, half:] = field[:, half:] + 0.5 * (even[...] - odd)


def lon_apply(here, blocks, matrices, extra=()):
    bands = len(blocks)
    band, _ = blocks[0].shape
    half = matrices[0].shape[0]
    return pl.pallas_call(
        functools.partial(lon_odd_kernel if extra else lon_even_kernel, bands),
        out_shape=jax.ShapeDtypeStruct((band, 2 * half if extra else half), jnp.float32),
        in_specs=[SMEM] + [VMEM] * (bands + 2 + len(extra)),
        out_specs=VMEM,
        scratch_shapes=[pltpu.VMEM((2 * band, half), jnp.bfloat16)],
        compiler_params=LIMIT,
        cost_estimate=pl.CostEstimate(
            flops=6 * band * half * half, bytes_accessed=4 * half * half, transcendentals=0
        ),
        name="lon_apply",
    )(here, *blocks, *matrices, *extra)


def multiplier_kernel(here_ref, own_ref, plus_ref, minus_ref, near_ref, cross_ref, out_ref):
    weight = weight_of(here_ref)
    half = own_ref.shape[1] // 2
    for at in range(0, own_ref.shape[0], ROWS):
        rows = slice(at, at + ROWS)
        plus, minus = plus_ref[rows] + weight(KNOWN) * (cross_ref[rows] - near_ref[rows]), minus_ref[rows]
        out_ref[rows, :half] = own_ref[rows, :half] - 0.5 * (plus + minus)
        out_ref[rows, half:] = own_ref[rows, half:] - 0.5 * (plus - minus)


def new_multipliers(here, own, *terms):
    band, width = own.shape
    rows = 4 * ROWS
    whole = pl.BlockSpec((rows, width), lambda i: (i, 0))
    part = pl.BlockSpec((rows, width // 2), lambda i: (i, 0))
    return pl.pallas_call(
        multiplier_kernel,
        grid=(band // rows,),
        out_shape=jax.ShapeDtypeStruct((band, width), jnp.float32),
        in_specs=[SMEM, whole] + [part] * 4,
        out_specs=whole,
        compiler_params=LIMIT,
        cost_estimate=pl.CostEstimate(flops=6 * band * width, bytes_accessed=20 * band * width, transcendentals=0),
        name="new_multipliers",
    )(here, own, *terms)


def exchange(blocks):
    bands = len(blocks)
    moved = [blocks[0]]
    for shift in range(1, bands):
        route = [(source, (source + shift) % bands) for source in range(bands)]
        moved.append(lax.ppermute(blocks[shift], "lat", route))
    return moved


def hop(value, pairs):
    return lax.ppermute(value, "win", pairs)


def per_device(
    state, multipliers, observations, obs_mask, speed, drift, kappa, lat_spectrum, lon_spectrum
):
    bands, windows = lax.axis_size("lat"), lax.axis_size("win")
    band, nlon = state.shape[2:]
    columns = nlon // 2 // bands
    if windows != 4 or state.shape[1] != 1 or bands % 2 or band % LANES or columns % LANES:
        return per_device_any(
            state, multipliers, observations, obs_mask, speed, drift, kappa, lat_spectrum, lon_spectrum
        )
    return per_device_hops(
        state, multipliers, observations, obs_mask, speed, drift, kappa, lat_spectrum, lon_spectrum
    )


def per_device_hops(
    state, multipliers, observations, obs_mask, speed, drift, kappa, lat_spectrum, lon_spectrum
):
    bands = lax.axis_size("lat")
    here = jnp.stack([lax.axis_index("lat"), lax.axis_index("win")]).astype(jnp.int32)
    x, mult = state[0, 0], multipliers[0, 0]
    edges = (
        lax.ppermute(x[-2:], "lat", [(i, i + 1) for i in range(bands - 1)]),
        lax.ppermute(x[:2], "lat", [(i + 1, i) for i in range(bands - 1)]),
    )
    x, own, x1, plus, minus, near, side = forecast(here, bands, (speed, drift, kappa), x, mult, edges)
    near = hop(near, [(0, 1), (1, 0), (2, 3)])
    side = hop(side, [(0, 2), (1, 3)])
    base_plus, base_minus, step_plus, second, third = defect(
        here, own, observations[0, :, 0], obs_mask[0], x1, plus, minus
    )
    far = hop(mix(here, None, near, step_plus), [(0, 2), (1, 3)])
    cross = hop(mix(here, SECOND, second, side), [(0, 1), (2, 3), (3, 2)])
    third = hop(third, [(0, 1), (1, 3)])
    plus = hop(plus, [(1, 2), (2, 3)])
    minus = hop(minus, [(0, 1), (1, 2), (2, 3)])
    lat_matrices = build(lat_spectrum)
    lon_matrices = build(lon_spectrum)
    even = resid_blocks(here, bands, EVEN, base_plus, near, far, cross)
    odd = resid_blocks(here, bands, ODD, base_minus, side, cross, third)
    even, odd = exchange(even), exchange(odd)
    even = lat_apply(here, even, lat_matrices)
    even, odd = exchange(even), exchange(lat_apply(here, odd, lat_matrices))
    even = lon_apply(here, even, lon_matrices[:2])
    field = lon_apply(here, odd, lon_matrices[2:], (even, x))
    lam = new_multipliers(here, own, plus, minus, near, cross)
    return (field[None, None], lam[None, None])


def solution(mesh):
    return jax.shard_map(
        per_device,
        mesh=mesh,
        in_specs=(
            P("win", None, "lat", None),
            P("win", None, "lat", None),
            P("win", None, None, "lat", None),
            P("win", None, "lat", None),
            P(),
            P(),
            P(),
            P(),
            P(),
        ),
        out_specs=(P("win", None, "lat", None), P("win", None, "lat", None)),
        check_vma=False,
    )
```

```python
import functools
import math

import numpy as np
import jax
import jax.numpy as jnp
from jax import lax
from jax.experimental import pallas as pl
from jax.experimental.pallas import tpu as pltpu
from jax.sharding import PartitionSpec as P


LANES = 128
ROWS = 8
WEIGHTS = (
    (0.0, 1.0, -1.0, 1.0, 0.5, 1.0, 0.0, 0.0, 0.0, 0.0, 0.0, 0.0, 0.0, 0.0),
    (0.5, 1 / 2, 1.0, 0.0, 1.0, 0.0, 0.0, 0.0, 0.0, 1.0, 0.0, 0.0, 1.0, 0.5),
    (0.5, 1 / 3, 1.0, 0.0, 0.0, 1.0, 1 / 3, 0.0, 1.0, 0.0, 0.5, 1.0, 0.0, 0.0),
    (0.5, 1 / 4, 1.0, 0.0, 0.0, 0.0, 1.0, 1.0, 1 / 3, 0.0, 0.0, 1.0, 1 / 3, 0.0),
)
OWN, SHARE, SIGN, FIRST, ONWARD, SECOND, SIDE, EVEN, ODD, KNOWN = 0, 1, 2, 3, 4, 5, 6, 7, 10, 13
VMEM = pl.BlockSpec(memory_space=pltpu.VMEM)
SMEM = pl.BlockSpec(memory_space=pltpu.SMEM)
ANY = pl.BlockSpec(memory_space=pl.ANY)
HBM = pl.BlockSpec(memory_space=pltpu.HBM)
LIMIT = pltpu.CompilerParams(vmem_limit_bytes=16 * 2**20)


def trig_tables(count):
    low = count // LANES
    blocks = low // 2
    turn = 2.0 * math.pi
    fine = np.arange(LANES)
    coarse = np.arange(low)
    inner = turn * ((coarse[:, None] * fine[None, :]) % low) / low
    middle = turn * (((fine // low)[:, None] * fine[None, :]) % LANES) / LANES
    member = (coarse[:, None] == (fine % low)[None, :]).astype(np.float32)
    twist = turn * (coarse[:, None] * fine[None, :]) / count
    outer = turn * ((np.arange(blocks)[:, None] * coarse[None, :]) % low) / low
    even = (coarse % 2 == 0)[None, :]
    keep = np.concatenate([np.broadcast_to(even, outer.shape), np.broadcast_to(~even, outer.shape)])
    outer = np.concatenate([outer, outer])
    pack = lambda angle, scale: np.concatenate([np.cos(angle), np.sin(angle)], axis=1) * scale
    return (pack(inner, 1.0).astype(np.float32), pack(middle, 1.0).astype(np.float32), member, pack(twist, 1.0 / count).astype(np.float32),
            (np.cos(outer) * keep).astype(np.float32), (np.sin(outer) * keep).astype(np.float32))


def build_kernel(count, d_ref, inner_ref, middle_ref, member_ref, twist_ref, cos_ref, sin_ref, even_hi, even_lo, odd_hi, odd_lo, toep, hank):
    blocks = count // LANES // 2
    high = lax.Precision.HIGHEST
    mm = functools.partial(jnp.dot, precision=high, preferred_element_type=jnp.float32)

    def turned(value, table):
        real, imag = value[:, :LANES], value[:, LANES:]
        tc, ts = table[:, :LANES], table[:, LANES:]
        return jnp.concatenate([real * tc - imag * ts, real * ts + imag * tc], axis=1)

    spectrum = jnp.concatenate([d_ref[:, at:at + LANES] for at in range(0, count, LANES)], axis=0)
    g = lax.dot_general(spectrum, inner_ref[...], (((0,), (0,)), ((), ())), precision=high,
                        preferred_element_type=jnp.float32)
    g = turned(mm(member_ref[...], turned(g, middle_ref)), twist_ref)
    gc, gs = g[:, :LANES], g[:, LANES:]
    c = mm(cos_ref[...], gc) - mm(sin_ref[...], gs)
    s = mm(sin_ref[...], gc) + mm(cos_ref[...], gs)
    upside_down = ROWS - 1 - lax.broadcasted_iota(jnp.int32, (ROWS, LANES), 0)
    ahead = (lax.broadcasted_iota(jnp.int32, (LANES, LANES), 1)
             - lax.broadcasted_iota(jnp.int32, (LANES, LANES), 0))
    for part in range(2):
        wrap = 1.0 if part == 0 else -1.0
        hi_ref, lo_ref = (even_hi, even_lo) if part == 0 else (odd_hi, odd_lo)

        def sheared(table, at, shift):
            at += part * blocks
            return pltpu.roll(jnp.broadcast_to(table[at:at + 1], (LANES, LANES)), shift, 1, stride=1, stride_axis=0)

        before = wrap * sheared(c, blocks - 1, 0)
        for b in range(blocks):
            now = sheared(c, b, 0)
            block = jnp.where(ahead >= 0, now, before)
            toep[b] = block
            toep[b + blocks] = wrap * block
            before = now
        first = now = sheared(s, 0, 1)
        for b in range(blocks):
            after = sheared(s, b + 1, 1) if b + 1 < blocks else wrap * first
            block = jnp.where(ahead <= 0, now, after)
            for at in range(0, LANES, ROWS):
                rows = jnp.take_along_axis(block[at:at + ROWS], upside_down, axis=0)
                hank[b, LANES - ROWS - at:LANES - at] = rows
                hank[b + blocks, LANES - ROWS - at:LANES - at] = wrap * rows
            now = after

        def body(i, _):
            for j in range(blocks):
                a = toep[jnp.where(j < i, j - i + 2 * blocks, j - i)] + hank[i + j]
                hi = a.astype(jnp.bfloat16)
                at = (pl.ds(pl.multiple_of(i * LANES, LANES), LANES), pl.ds(j * LANES, LANES))
                hi_ref[at] = hi
                lo_ref[at] = (a - hi.astype(jnp.float32)).astype(jnp.bfloat16)
            return 0

        lax.fori_loop(0, blocks, body, 0)


def build(spectrum):
    count = spectrum.shape[1]
    half = count // 2
    tables = trig_tables(count)
    shape = jax.ShapeDtypeStruct((half, half), jnp.bfloat16)
    return pl.pallas_call(
        functools.partial(build_kernel, count),
        out_shape=[shape] * 4, in_specs=[VMEM] * 7, out_specs=[VMEM] * 4,
        scratch_shapes=[pltpu.VMEM((2 * half // LANES, LANES, LANES), jnp.float32)] * 2,
        compiler_params=LIMIT,
        cost_estimate=pl.CostEstimate(flops=2 * half * half * 8, bytes_accessed=8 * half * half, transcendentals=0),
    )(spectrum, *tables)


def extended(block, sides, width):
    for axis, dim in sides:
        count = lax.axis_size(axis)
        forward = [(i, i + 1) for i in range(count - 1)]
        backward = [(target, source) for source, target in forward]
        low = lax.ppermute(
            lax.slice_in_dim(block, block.shape[dim] - width, None, axis=dim), axis, forward
        )
        high = lax.ppermute(lax.slice_in_dim(block, 0, width, axis=dim), axis, backward)
        block = jnp.concatenate([low, block, high], axis=dim)
    return block


def passed_along(value, axis, steps):
    count = lax.axis_size(axis)
    first, last = (max(0, -steps), min(count, count - steps))
    return lax.ppermute(value, axis, [(source, source + steps) for source in range(first, last)])


def prefix(array, axis, combine, identity):
    peers, here = (lax.axis_size(axis), lax.axis_index(axis))
    everything = lax.all_gather(array, axis)
    start = jnp.broadcast_to(jnp.asarray(identity, array.dtype), array.shape)

    def turn(k, before):
        reached = k < here
        new = combine(before, everything[k])
        return jnp.where(reached, new, before)

    return lax.fori_loop(0, peers, turn, start)


def hartley(count):
    index = jnp.arange(count, dtype=jnp.int32)
    product = index[:, None] * index[None, :] % count
    angle = product.astype(jnp.float32) * (2.0 * math.pi / count)
    return jnp.cos(angle) + jnp.sin(angle)


def advance(padded, speed, drift, kappa):
    field = padded[:, 1:-1]
    north = padded[:, 2:]
    south = padded[:, :-2]
    east = jnp.roll(field, -1, axis=-1)
    west = jnp.roll(field, 1, axis=-1)
    speed_c = speed[:, None, None]
    drift_c = drift[:, None, None]
    kappa_c = kappa[:, None, None]
    return (
        field
        - speed_c * field * (east - west) * 0.5
        - drift_c * (north - south) * 0.5
        + kappa_c * (east + west + north + south - 4.0 * field)
    )


def per_device_any(
    state, multipliers, observations, obs_mask, speed, drift, kappa, lat_spectrum, lon_spectrum
):
    high = lax.Precision.HIGHEST
    field = state[0]
    lam = multipliers[0]
    observed = observations[0]
    mask = obs_mask[0].astype(jnp.float32)
    band = field.shape[1]
    nlon = field.shape[2]
    bands = lax.axis_size("lat")
    nlat = band * bands
    columns = nlon // bands
    lat_index = lax.axis_index("lat")
    win_index = lax.axis_index("win")
    h_lon = hartley(nlon)
    h_lat = hartley(nlat)
    lon_part = lax.dynamic_slice_in_dim(lon_spectrum, lat_index * columns, columns, 1)
    weight = lat_spectrum[:, :, None] * lon_part[:, None, :]
    divisor = jnp.maximum(win_index, 1).astype(jnp.float32)
    rows_global = lat_index * band + jnp.arange(-1, band + 1, dtype=jnp.int32)
    inside = ((rows_global >= 0) & (rows_global < nlat))[None, :, None]
    padded = extended(field, (("lat", 1),), 2)
    widened = advance(padded, speed, drift, kappa)
    widened = jnp.where(inside, widened, jnp.float32(0.0))
    first = widened[:, 1:-1]
    second = advance(widened, speed, drift, kappa)
    defect = mask[0][None] * (observed[0] - first) + mask[1][None] * (observed[1] - second)
    prior_end = passed_along(second, "win", 1)
    mismatch = jnp.where(win_index > 0, field - prior_end, jnp.float32(0.0))
    lam = lam + 0.5 * mismatch
    carried = prefix(lam, "win", lambda earlier, later: earlier + later, jnp.zeros_like(lam))
    resid = defect + lam - carried / divisor
    spectral = jnp.matmul(resid, h_lon, precision=high)
    spectral = lax.all_to_all(spectral, "lat", split_axis=2, concat_axis=1, tiled=True)
    spectral = jnp.einsum("ij,ljk->lik", h_lat, spectral, precision=high) * weight
    spectral = jnp.einsum("ij,ljk->lik", h_lat, spectral, precision=high)
    spectral = lax.all_to_all(spectral, "lat", split_axis=1, concat_axis=2, tiled=True)
    increment = jnp.matmul(spectral, h_lon, precision=high) / (nlat * nlon)
    field = field + 0.5 * increment
    return (field[None], lam[None])


def split(value):
    hi = value.astype(jnp.bfloat16)
    return hi, (value - hi.astype(jnp.float32)).astype(jnp.bfloat16)


def stencil(scal, field, north, south):
    width = field.shape[1]
    east = pltpu.roll(field, width - 1, 1)
    west = pltpu.roll(field, 1, 1)
    return (
        field
        - scal[0] * field * (east - west) * 0.5
        - scal[1] * (north - south) * 0.5
        + scal[2] * (east + west + north + south - 4.0 * field)
    )


def weight_of(here_ref):
    def pick(number):
        value = WEIGHTS[0][number]
        for window in range(1, len(WEIGHTS)):
            value = jnp.where(here_ref[1] == window, WEIGHTS[window][number], value)
        return value

    return pick


def windowed(sign, share, own, ended):
    half = own.shape[1] // 2
    values = (ended, sign * ended + share * own)
    return [part for value in values for part in
            (value[:, :half] + value[:, half:], value[:, :half] - value[:, half:])]


def forecast_kernel(here_ref, model, x_hbm, mult_hbm, x_ref, own_ref, x1_ref, *refs):
    outs, (mult_ref, sems) = refs[:4], refs[4:]
    band = x_ref.shape[0]
    chunk = band // 4
    weight, scal = weight_of(here_ref), (model[0], model[1], model[2])
    sign, share = weight(SIGN), weight(SHARE)

    def step(source, at, count):
        return stencil(scal, source[at:at + count], source[at + 1:at + count + 1], source[at - 1:at + count - 1])

    copies = []
    for number, (source, target) in enumerate(((x_hbm, x_ref), (mult_hbm, mult_ref))):
        for part in range(4):
            rows = slice(part * chunk, (part + 1) * chunk)
            copies.append(pltpu.make_async_copy(source.at[rows], target.at[rows], sems.at[number, part]))
            copies[-1].start()
    ready, stepped = 0, ROWS
    for part in range(4):
        copies[part].wait()
        ready += chunk
        if part == 0:
            x1_ref[ROWS - 1:ROWS] = step(x_ref, ROWS - 1, 1)
        while stepped + ROWS < ready:
            x1_ref[stepped:stepped + ROWS] = step(x_ref, stepped, ROWS)
            stepped += ROWS
    x1_ref[stepped:stepped + 1] = step(x_ref, stepped, 1)
    kept = weight(OWN)
    for part in range(4):
        copies[4 + part].wait()
        for at in range(part * chunk, (part + 1) * chunk, ROWS):
            rows = slice(at, at + ROWS)
            own = mult_ref[rows] + kept * x_ref[rows]
            own_ref[rows] = own
            if 0 < at < band - ROWS:
                for out, value in zip(outs, windowed(sign, share, own, 0.5 * step(x1_ref, at, ROWS))):
                    out[rows] = value


def edge_kernel(bands, here_ref, model, x_ref, own_ref, low_ref, high_ref, *refs):
    outs, (ext, mid, whole, parts, sems) = refs[5:10], refs[10:]
    band = x_ref.shape[0]
    edge = low_ref.shape[0]
    weight, scal = weight_of(here_ref), (model[0], model[1], model[2])
    sign, share = weight(SIGN), weight(SHARE)
    copies = []
    for end in range(2):
        at = 0 if end == 0 else band - ROWS
        if end == 0:
            ext[end, ROWS - edge:ROWS] = low_ref[...]
            ext[end, ROWS:3 * ROWS] = x_ref[:2 * ROWS]
        else:
            ext[end, :2 * ROWS] = x_ref[band - 2 * ROWS:]
            ext[end, 2 * ROWS:2 * ROWS + edge] = high_ref[...]

        def step(source, row, count):
            return stencil(scal, source[end, row:row + count], source[end, row + 1:row + count + 1],
                           source[end, row - 1:row + count - 1])

        before, after = step(ext, ROWS - 1, 1), step(ext, 2 * ROWS, 1)
        if end == 0:
            before = before * jnp.where(here_ref[0] > 0, 1.0, 0.0)
        else:
            after = after * jnp.where(here_ref[0] < bands - 1, 1.0, 0.0)
        mid[end, ROWS - 1:ROWS] = before
        mid[end, 2 * ROWS:2 * ROWS + 1] = after
        mid[end, ROWS:2 * ROWS] = step(ext, ROWS, ROWS)
        rows = slice(at, at + ROWS)
        whole[end] = mid[end, ROWS:2 * ROWS]
        for number, part in enumerate(windowed(sign, share, own_ref[rows], 0.5 * step(mid, ROWS, ROWS))):
            parts[end, number] = part
        sources = [whole.at[end]] + [parts.at[end, number] for number in range(4)]
        for number, (source, out) in enumerate(zip(sources, outs)):
            copies.append(pltpu.make_async_copy(source, out.at[rows], sems.at[end, number]))
            copies[-1].start()
    for copy in copies:
        copy.wait()


def forecast(here, bands, model, x, mult, exchange_edges):
    band, width = x.shape
    whole = jax.ShapeDtypeStruct((band, width), jnp.float32)
    shapes = [whole] + [jax.ShapeDtypeStruct((band, width // 2), jnp.float32)] * 4
    x, own, *inner = pl.pallas_call(
        forecast_kernel,
        out_shape=[whole] * 2 + shapes,
        in_specs=[SMEM] * 2 + [HBM] * 2,
        out_specs=[VMEM] * 7,
        scratch_shapes=[pltpu.VMEM((band, width), jnp.float32), pltpu.SemaphoreType.DMA((2, 4))],
        compiler_params=LIMIT,
        cost_estimate=pl.CostEstimate(flops=40 * band * width, bytes_accessed=20 * band * width, transcendentals=0),
        name="forecast",
    )(here, model, pltpu.with_memory_space_constraint(x, pltpu.HBM), pltpu.with_memory_space_constraint(mult, pltpu.HBM))
    low, high = exchange_edges
    outs = pl.pallas_call(
        functools.partial(edge_kernel, bands),
        out_shape=shapes,
        in_specs=[SMEM] * 2 + [VMEM] * 4 + [ANY] * 5,
        out_specs=[ANY] * 5,
        input_output_aliases={6 + number: number for number in range(5)},
        scratch_shapes=[pltpu.VMEM((2, 4 * ROWS, width), jnp.float32)] * 2 + [
            pltpu.VMEM((2, ROWS, width), jnp.float32),
            pltpu.VMEM((2, 4, ROWS, width // 2), jnp.float32),
            pltpu.SemaphoreType.DMA((2, 5)),
        ],
        compiler_params=LIMIT,
        cost_estimate=pl.CostEstimate(flops=1000 * width, bytes_accessed=400 * width, transcendentals=0),
        name="edges",
    )(here, model, x, own, low, high, *inner)
    return x, own, *outs


def defect_kernel(here_ref, own_ref, obs_ref, mask_ref, x1_ref, plus_ref, minus_ref,
                  base_plus, base_minus, step_plus, second_ref, third_ref):
    half = own_ref.shape[1] // 2
    weight = weight_of(here_ref)
    first, share = weight(FIRST) > 0.0, weight(SHARE)
    for at in range(0, own_ref.shape[0], ROWS):
        rows = slice(at, at + ROWS)
        plus, minus = plus_ref[rows], minus_ref[rows]
        base, own = [], []
        for cols, end in ((slice(0, half), plus + minus), (slice(half, 2 * half), plus - minus)):
            own.append(own_ref[rows, cols])
            seen = mask_ref[:, rows, cols].astype(jnp.float32)
            base.append(
                own[-1] + seen[0] * (obs_ref[0, rows, cols] - x1_ref[rows, cols])
                + seen[1] * (obs_ref[1, rows, cols] - end)
            )
        base_plus[rows] = base[0] + base[1]
        base_minus[rows] = base[0] - base[1]
        own_plus, own_minus = own[0] + own[1], own[0] - own[1]
        step_plus[rows] = own_plus - plus
        sent_minus = minus + share * own_minus
        second_ref[rows] = jnp.where(first, plus + share * own_plus, sent_minus)
        third_ref[rows] = jnp.where(first, sent_minus, own_minus - minus)


def defect(here, own, obs, mask, x1, plus, minus):
    band, width = own.shape
    rows = 4 * ROWS
    whole = pl.BlockSpec((rows, width), lambda i: (i, 0))
    pair = pl.BlockSpec((2, rows, width), lambda i: (0, i, 0))
    part = pl.BlockSpec((rows, width // 2), lambda i: (i, 0))
    return pl.pallas_call(
        defect_kernel,
        grid=(band // rows,),
        out_shape=[jax.ShapeDtypeStruct((band, width // 2), jnp.float32)] * 5,
        in_specs=[SMEM, whole, pair, pair, whole, part, part],
        out_specs=[part] * 5,
        compiler_params=LIMIT,
        cost_estimate=pl.CostEstimate(flops=30 * band * width, bytes_accessed=40 * band * width, transcendentals=0),
        name="defect",
    )(here, own, obs, mask, x1, plus, minus)


def mix_kernel(first, here_ref, one_ref, other_ref, out_ref):
    weight = weight_of(here_ref)
    one = one_ref[...] if first is None else weight(first) * one_ref[...]
    out_ref[...] = one + weight(ONWARD if first is None else SIDE) * other_ref[...]


def mix(here, first, one, other):
    return pl.pallas_call(
        functools.partial(mix_kernel, first),
        out_shape=jax.ShapeDtypeStruct(one.shape, jnp.float32),
        in_specs=[SMEM] + [VMEM] * 2,
        out_specs=VMEM,
        compiler_params=LIMIT,
        cost_estimate=pl.CostEstimate(flops=3 * one.size, bytes_accessed=12 * one.size, transcendentals=0),
        name="mix",
    )(here, one, other)


def resid_kernel(bands, first, here_ref, base_ref, *refs):
    terms, outs = refs[:-bands], refs[-bands:]
    weights = [weight_of(here_ref)(first + number) for number in range(len(terms))]
    columns = outs[0].shape[1]
    for shift in range(bands):
        target = lax.rem(here_ref[0] + shift, bands)
        at = pl.ds(pl.multiple_of(target * columns, columns), columns)
        value = base_ref[:, at]
        for weight, term in zip(weights, terms):
            value = value - weight * term[:, at]
        outs[shift][...] = value


def resid_blocks(here, bands, first, base, *terms):
    band, half = base.shape
    columns = half // bands
    return pl.pallas_call(
        functools.partial(resid_kernel, bands, first),
        out_shape=[jax.ShapeDtypeStruct((band, columns), jnp.float32)] * bands,
        in_specs=[SMEM] + [VMEM] * 4,
        out_specs=[VMEM] * bands,
        compiler_params=LIMIT,
        cost_estimate=pl.CostEstimate(flops=8 * band * half, bytes_accessed=24 * band * half, transcendentals=0),
        name="resid_blocks",
    )(here, base, *terms)


def lat_kernel(bands, here_ref, *refs):
    blocks, (ehi, elo, ohi, olo) = refs[:bands], refs[bands:bands + 4]
    outs, (gathered, mixed) = refs[bands + 4:2 * bands + 4], refs[2 * bands + 4:]
    here = here_ref[0]
    pairs = bands // 2
    band, columns = blocks[0].shape
    for shift in range(pairs):
        source = lax.rem(here - shift + bands, bands)
        rows = pl.ds(pl.multiple_of(lax.rem(source, pairs) * band, band), band)
        first, other = blocks[shift][...], blocks[shift + pairs][...]
        sign = jnp.where(source < pairs, 1.0, -1.0)
        for part, value in enumerate((first + other, (first - other) * sign)):
            hi, lo = split(value)
            gathered[part, rows, :columns] = hi
            gathered[part, rows, columns:] = lo
    dot = functools.partial(jnp.dot, preferred_element_type=jnp.float32)
    for part, (hi, lo) in enumerate(((ehi, elo), (ohi, olo))):
        both = dot(hi[...], gathered[part])
        mixed[part] = both[:, :columns] + both[:, columns:] + dot(lo[...], gathered[part, :, :columns])
    for shift in range(bands):
        target = lax.rem(here + shift, bands)
        rows = pl.ds(pl.multiple_of(lax.rem(target, pairs) * band, band), band)
        sign = jnp.where(target < pairs, 1.0, -1.0)
        outs[shift][...] = mixed[0, rows] + sign * mixed[1, rows]


def lat_apply(here, blocks, matrices):
    bands = len(blocks)
    band, columns = blocks[0].shape
    half = matrices[0].shape[0]
    return pl.pallas_call(
        functools.partial(lat_kernel, bands),
        out_shape=[jax.ShapeDtypeStruct((band, columns), jnp.float32)] * bands,
        in_specs=[SMEM] + [VMEM] * (bands + 4),
        out_specs=[VMEM] * bands,
        scratch_shapes=[
            pltpu.VMEM((2, half, 2 * columns), jnp.bfloat16),
            pltpu.VMEM((2, half, columns), jnp.float32),
        ],
        compiler_params=LIMIT,
        cost_estimate=pl.CostEstimate(
            flops=12 * half * half * columns, bytes_accessed=8 * half * half, transcendentals=0
        ),
        name="lat_apply",
    )(here, *blocks, *matrices)


def gather_rows(here, bands, blocks, gathered):
    band, columns = blocks[0].shape
    for shift in range(bands):
        source = lax.rem(here - shift + bands, bands)
        at = pl.ds(pl.multiple_of(source * columns, columns), columns)
        hi, lo = split(blocks[shift][...])
        gathered[:band, at] = hi
        gathered[band:, at] = lo


def lon_product(band, hi, lo, gathered):
    dot = functools.partial(jnp.dot, preferred_element_type=jnp.float32)
    both = dot(gathered[...], hi[...])
    return both[:band] + both[band:] + dot(gathered[:band], lo[...])


def lon_even_kernel(bands, here_ref, *refs):
    blocks, (hi, lo, out, gathered) = refs[:bands], refs[bands:]
    gather_rows(here_ref[0], bands, blocks, gathered)
    out[...] = lon_product(blocks[0].shape[0], hi, lo, gathered)


def lon_odd_kernel(bands, here_ref, *refs):
    blocks, (hi, lo, even, field, out, gathered, result, sems) = refs[:bands], refs[bands:]
    gather_rows(here_ref[0], bands, blocks, gathered)
    half = hi.shape[0]
    band, parts = blocks[0].shape[0], sems.shape[0]
    chunk = half // parts
    copies = []
    for part in range(parts):
        cols = slice(part * chunk, (part + 1) * chunk)
        odd = lon_product(band, hi.at[:, cols], lo.at[:, cols], gathered)
        for side, value in enumerate((even[:, cols] + odd, even[:, cols] - odd)):
            at = slice(side * half + part * chunk, side * half + (part + 1) * chunk)
            result[:, at] = field[:, at] + 0.5 * value
            copies.append(pltpu.make_async_copy(result.at[:, at], out.at[:, at], sems.at[part, side]))
            copies[-1].start()
    for copy in copies:
        copy.wait()


def lon_apply(here, blocks, matrices, extra=()):
    bands = len(blocks)
    band, _ = blocks[0].shape
    half = matrices[0].shape[0]
    scratch = [pltpu.VMEM((2 * band, half), jnp.bfloat16)]
    if extra:
        scratch += [pltpu.VMEM((band, 2 * half), jnp.float32), pltpu.SemaphoreType.DMA((4, 2))]
    return pl.pallas_call(
        functools.partial(lon_odd_kernel if extra else lon_even_kernel, bands),
        out_shape=jax.ShapeDtypeStruct((band, 2 * half if extra else half), jnp.float32),
        in_specs=[SMEM] + [VMEM] * (bands + 2 + len(extra)),
        out_specs=ANY if extra else VMEM,
        scratch_shapes=scratch,
        compiler_params=LIMIT,
        cost_estimate=pl.CostEstimate(
            flops=6 * band * half * half, bytes_accessed=4 * half * half, transcendentals=0
        ),
        name="lon_apply",
    )(here, *blocks, *matrices, *extra)


def multiplier_kernel(here_ref, own_ref, plus_ref, minus_ref, near_ref, direct_ref, out_ref, result, sems):
    known = weight_of(here_ref)(KNOWN)
    band, half = plus_ref.shape
    chunk = band // sems.shape[0]
    copies = []
    for at in range(0, band, ROWS):
        rows = slice(at, at + ROWS)
        plus, minus = plus_ref[rows] + known * (direct_ref[rows] - near_ref[rows]), minus_ref[rows]
        result[rows, :half] = own_ref[rows, :half] - 0.5 * (plus + minus)
        result[rows, half:] = own_ref[rows, half:] - 0.5 * (plus - minus)
        if (at + ROWS) % chunk == 0:
            part = slice(at + ROWS - chunk, at + ROWS)
            copies.append(pltpu.make_async_copy(result.at[part], out_ref.at[part], sems.at[at // chunk]))
            copies[-1].start()
    for copy in copies:
        copy.wait()


def new_multipliers(here, own, *terms):
    band, width = own.shape
    return pl.pallas_call(
        multiplier_kernel,
        out_shape=jax.ShapeDtypeStruct((band, width), jnp.float32),
        in_specs=[SMEM] + [VMEM] * 5,
        out_specs=ANY,
        scratch_shapes=[pltpu.VMEM((band, width), jnp.float32), pltpu.SemaphoreType.DMA((4,))],
        compiler_params=LIMIT,
        cost_estimate=pl.CostEstimate(flops=6 * band * width, bytes_accessed=20 * band * width, transcendentals=0),
        name="new_multipliers",
    )(here, own, *terms)


def exchange(blocks):
    bands = len(blocks)
    moved = [blocks[0]]
    for shift in range(1, bands):
        route = [(source, (source + shift) % bands) for source in range(bands)]
        moved.append(lax.ppermute(blocks[shift], "lat", route))
    return moved


def hop(value, pairs):
    return lax.ppermute(value, "win", pairs)


def per_device(
    state, multipliers, observations, obs_mask, speed, drift, kappa, lat_spectrum, lon_spectrum
):
    bands, windows = lax.axis_size("lat"), lax.axis_size("win")
    band, nlon = state.shape[2:]
    columns = nlon // 2 // bands
    if windows != 4 or state.shape[1] != 1 or bands % 2 or band % LANES or columns % LANES:
        return per_device_any(
            state, multipliers, observations, obs_mask, speed, drift, kappa, lat_spectrum, lon_spectrum
        )
    return per_device_hops(
        state, multipliers, observations, obs_mask, speed, drift, kappa, lat_spectrum, lon_spectrum
    )


def per_device_hops(
    state, multipliers, observations, obs_mask, speed, drift, kappa, lat_spectrum, lon_spectrum
):
    bands = lax.axis_size("lat")
    here = jnp.stack([lax.axis_index("lat"), lax.axis_index("win")]).astype(jnp.int32)
    x, mult = state[0, 0], multipliers[0, 0]
    edges = (
        lax.ppermute(x[-2:], "lat", [(i, i + 1) for i in range(bands - 1)]),
        lax.ppermute(x[:2], "lat", [(i + 1, i) for i in range(bands - 1)]),
    )
    x, own, x1, plus, minus, near, side = forecast(here, bands, jnp.concatenate([speed, drift, kappa]), x, mult, edges)
    near = hop(near, [(0, 1), (1, 0), (2, 3)])
    side = hop(side, [(0, 2), (1, 3)])
    base_plus, base_minus, step_plus, second, third = defect(
        here, own, observations[0, :, 0], obs_mask[0], x1, plus, minus
    )
    direct = hop(second, [(0, 1)])
    far = hop(mix(here, None, near, step_plus), [(0, 2), (1, 3)])
    cross = hop(mix(here, SECOND, second, side), [(2, 3), (3, 2)])
    third = hop(third, [(0, 1), (1, 3)])
    plus = hop(plus, [(1, 2), (2, 3)])
    minus = hop(minus, [(0, 1), (1, 2), (2, 3)])
    lat_matrices = build(lat_spectrum)
    lon_matrices = build(lon_spectrum)
    even = resid_blocks(here, bands, EVEN, base_plus, near, far, direct)
    odd = resid_blocks(here, bands, ODD, base_minus, side, cross, third)
    even, odd = exchange(even), exchange(odd)
    even = lat_apply(here, even, lat_matrices)
    even, odd = exchange(even), exchange(lat_apply(here, odd, lat_matrices))
    even = lon_apply(here, even, lon_matrices[:2])
    field = lon_apply(here, odd, lon_matrices[2:], (even, x))
    lam = new_multipliers(here, own, plus, minus, near, direct)
    return (field[None, None], lam[None, None])


def solution(mesh):
    return jax.shard_map(
        per_device,
        mesh=mesh,
        in_specs=(
            P("win", None, "lat", None),
            P("win", None, "lat", None),
            P("win", None, None, "lat", None),
            P("win", None, "lat", None),
            P(),
            P(),
            P(),
            P(),
            P(),
        ),
        out_specs=(P("win", None, "lat", None), P("win", None, "lat", None)),
        check_vma=False,
    )
```

```python
import functools
import math

import numpy as np
import jax
import jax.numpy as jnp
from jax import lax
from jax.experimental import pallas as pl
from jax.experimental.pallas import tpu as pltpu
from jax.sharding import PartitionSpec as P


LANES = 128
ROWS = 8
WEIGHTS = (
    (0.0, 1.0, -1.0, 1.0, 0.5, 1.0, 0.0, 0.0, 0.0, 0.0, 0.0, 0.0, 0.0, 0.0),
    (0.5, 1 / 2, 1.0, 0.0, 1.0, 0.0, 0.0, 0.0, 0.0, 1.0, 0.0, 0.0, 1.0, 0.5),
    (0.5, 1 / 3, 1.0, 0.0, 0.0, 1.0, 1 / 3, 0.0, 1.0, 0.0, 0.5, 1.0, 0.0, 0.0),
    (0.5, 1 / 4, 1.0, 0.0, 0.0, 0.0, 1.0, 1.0, 1 / 3, 0.0, 0.0, 1.0, 1 / 3, 0.0),
)
OWN, SHARE, SIGN, FIRST, ONWARD, SECOND, SIDE, EVEN, ODD, KNOWN = 0, 1, 2, 3, 4, 5, 6, 7, 10, 13
VMEM = pl.BlockSpec(memory_space=pltpu.VMEM)
SMEM = pl.BlockSpec(memory_space=pltpu.SMEM)
ANY = pl.BlockSpec(memory_space=pl.ANY)
HBM = pl.BlockSpec(memory_space=pltpu.HBM)
LIMIT = pltpu.CompilerParams(vmem_limit_bytes=16 * 2**20)


def trig_tables(count):
    low = count // LANES
    blocks = low // 2
    turn = 2.0 * math.pi
    fine = np.arange(LANES)
    coarse = np.arange(low)
    inner = turn * ((coarse[:, None] * fine[None, :]) % low) / low
    middle = turn * (((fine // low)[:, None] * fine[None, :]) % LANES) / LANES
    member = (coarse[:, None] == (fine % low)[None, :]).astype(np.float32)
    twist = turn * (coarse[:, None] * fine[None, :]) / count
    outer = turn * ((np.arange(blocks)[:, None] * coarse[None, :]) % low) / low
    even = (coarse % 2 == 0)[None, :]
    keep = np.concatenate([np.broadcast_to(even, outer.shape), np.broadcast_to(~even, outer.shape)])
    outer = np.concatenate([outer, outer])
    pack = lambda angle, scale: np.concatenate([np.cos(angle), np.sin(angle)], axis=1) * scale
    return (pack(inner, 1.0).astype(np.float32), pack(middle, 1.0).astype(np.float32), member, pack(twist, 1.0 / count).astype(np.float32),
            (np.cos(outer) * keep).astype(np.float32), (np.sin(outer) * keep).astype(np.float32))


def build_kernel(count, d_ref, inner_ref, middle_ref, member_ref, twist_ref, cos_ref, sin_ref, even_hi, even_lo, odd_hi, odd_lo, toep, hank):
    blocks = count // LANES // 2
    high = lax.Precision.HIGHEST
    mm = functools.partial(jnp.dot, precision=high, preferred_element_type=jnp.float32)

    def turned(value, table):
        real, imag = value[:, :LANES], value[:, LANES:]
        tc, ts = table[:, :LANES], table[:, LANES:]
        return jnp.concatenate([real * tc - imag * ts, real * ts + imag * tc], axis=1)

    spectrum = jnp.concatenate([d_ref[:, at:at + LANES] for at in range(0, count, LANES)], axis=0)
    g = lax.dot_general(spectrum, inner_ref[...], (((0,), (0,)), ((), ())), precision=high,
                        preferred_element_type=jnp.float32)
    g = turned(mm(member_ref[...], turned(g, middle_ref)), twist_ref)
    gc, gs = g[:, :LANES], g[:, LANES:]
    c = mm(cos_ref[...], gc) - mm(sin_ref[...], gs)
    s = mm(sin_ref[...], gc) + mm(cos_ref[...], gs)
    upside_down = ROWS - 1 - lax.broadcasted_iota(jnp.int32, (ROWS, LANES), 0)
    ahead = (lax.broadcasted_iota(jnp.int32, (LANES, LANES), 1)
             - lax.broadcasted_iota(jnp.int32, (LANES, LANES), 0))
    for part in range(2):
        wrap = 1.0 if part == 0 else -1.0
        hi_ref, lo_ref = (even_hi, even_lo) if part == 0 else (odd_hi, odd_lo)

        def sheared(table, at, shift):
            at += part * blocks
            return pltpu.roll(jnp.broadcast_to(table[at:at + 1], (LANES, LANES)), shift, 1, stride=1, stride_axis=0)

        before = wrap * sheared(c, blocks - 1, 0)
        for b in range(blocks):
            now = sheared(c, b, 0)
            block = jnp.where(ahead >= 0, now, before)
            toep[b] = block
            toep[b + blocks] = wrap * block
            before = now
        first = now = sheared(s, 0, 1)
        for b in range(blocks):
            after = sheared(s, b + 1, 1) if b + 1 < blocks else wrap * first
            block = jnp.where(ahead <= 0, now, after)
            for at in range(0, LANES, ROWS):
                rows = jnp.take_along_axis(block[at:at + ROWS], upside_down, axis=0)
                hank[b, LANES - ROWS - at:LANES - at] = rows
                hank[b + blocks, LANES - ROWS - at:LANES - at] = wrap * rows
            now = after

        def body(i, _):
            for j in range(blocks):
                a = toep[jnp.where(j < i, j - i + 2 * blocks, j - i)] + hank[i + j]
                hi = a.astype(jnp.bfloat16)
                at = (pl.ds(pl.multiple_of(i * LANES, LANES), LANES), pl.ds(j * LANES, LANES))
                hi_ref[at] = hi
                lo_ref[at] = (a - hi.astype(jnp.float32)).astype(jnp.bfloat16)
            return 0

        lax.fori_loop(0, blocks, body, 0)


def build(spectrum):
    count = spectrum.shape[1]
    half = count // 2
    tables = trig_tables(count)
    shape = jax.ShapeDtypeStruct((half, half), jnp.bfloat16)
    return pl.pallas_call(
        functools.partial(build_kernel, count),
        out_shape=[shape] * 4, in_specs=[VMEM] * 7, out_specs=[VMEM] * 4,
        scratch_shapes=[pltpu.VMEM((2 * half // LANES, LANES, LANES), jnp.float32)] * 2,
        compiler_params=LIMIT,
        cost_estimate=pl.CostEstimate(flops=2 * half * half * 8, bytes_accessed=8 * half * half, transcendentals=0),
    )(spectrum, *tables)


def extended(block, sides, width):
    for axis, dim in sides:
        count = lax.axis_size(axis)
        forward = [(i, i + 1) for i in range(count - 1)]
        backward = [(target, source) for source, target in forward]
        low = lax.ppermute(
            lax.slice_in_dim(block, block.shape[dim] - width, None, axis=dim), axis, forward
        )
        high = lax.ppermute(lax.slice_in_dim(block, 0, width, axis=dim), axis, backward)
        block = jnp.concatenate([low, block, high], axis=dim)
    return block


def passed_along(value, axis, steps):
    count = lax.axis_size(axis)
    first, last = (max(0, -steps), min(count, count - steps))
    return lax.ppermute(value, axis, [(source, source + steps) for source in range(first, last)])


def prefix(array, axis, combine, identity):
    peers, here = (lax.axis_size(axis), lax.axis_index(axis))
    everything = lax.all_gather(array, axis)
    start = jnp.broadcast_to(jnp.asarray(identity, array.dtype), array.shape)

    def turn(k, before):
        reached = k < here
        new = combine(before, everything[k])
        return jnp.where(reached, new, before)

    return lax.fori_loop(0, peers, turn, start)


def hartley(count):
    index = jnp.arange(count, dtype=jnp.int32)
    product = index[:, None] * index[None, :] % count
    angle = product.astype(jnp.float32) * (2.0 * math.pi / count)
    return jnp.cos(angle) + jnp.sin(angle)


def advance(padded, speed, drift, kappa):
    field = padded[:, 1:-1]
    north = padded[:, 2:]
    south = padded[:, :-2]
    east = jnp.roll(field, -1, axis=-1)
    west = jnp.roll(field, 1, axis=-1)
    speed_c = speed[:, None, None]
    drift_c = drift[:, None, None]
    kappa_c = kappa[:, None, None]
    return (
        field
        - speed_c * field * (east - west) * 0.5
        - drift_c * (north - south) * 0.5
        + kappa_c * (east + west + north + south - 4.0 * field)
    )


def per_device_any(
    state, multipliers, observations, obs_mask, speed, drift, kappa, lat_spectrum, lon_spectrum
):
    high = lax.Precision.HIGHEST
    field = state[0]
    lam = multipliers[0]
    observed = observations[0]
    mask = obs_mask[0].astype(jnp.float32)
    band = field.shape[1]
    nlon = field.shape[2]
    bands = lax.axis_size("lat")
    nlat = band * bands
    columns = nlon // bands
    lat_index = lax.axis_index("lat")
    win_index = lax.axis_index("win")
    h_lon = hartley(nlon)
    h_lat = hartley(nlat)
    lon_part = lax.dynamic_slice_in_dim(lon_spectrum, lat_index * columns, columns, 1)
    weight = lat_spectrum[:, :, None] * lon_part[:, None, :]
    divisor = jnp.maximum(win_index, 1).astype(jnp.float32)
    rows_global = lat_index * band + jnp.arange(-1, band + 1, dtype=jnp.int32)
    inside = ((rows_global >= 0) & (rows_global < nlat))[None, :, None]
    padded = extended(field, (("lat", 1),), 2)
    widened = advance(padded, speed, drift, kappa)
    widened = jnp.where(inside, widened, jnp.float32(0.0))
    first = widened[:, 1:-1]
    second = advance(widened, speed, drift, kappa)
    defect = mask[0][None] * (observed[0] - first) + mask[1][None] * (observed[1] - second)
    prior_end = passed_along(second, "win", 1)
    mismatch = jnp.where(win_index > 0, field - prior_end, jnp.float32(0.0))
    lam = lam + 0.5 * mismatch
    carried = prefix(lam, "win", lambda earlier, later: earlier + later, jnp.zeros_like(lam))
    resid = defect + lam - carried / divisor
    spectral = jnp.matmul(resid, h_lon, precision=high)
    spectral = lax.all_to_all(spectral, "lat", split_axis=2, concat_axis=1, tiled=True)
    spectral = jnp.einsum("ij,ljk->lik", h_lat, spectral, precision=high) * weight
    spectral = jnp.einsum("ij,ljk->lik", h_lat, spectral, precision=high)
    spectral = lax.all_to_all(spectral, "lat", split_axis=1, concat_axis=2, tiled=True)
    increment = jnp.matmul(spectral, h_lon, precision=high) / (nlat * nlon)
    field = field + 0.5 * increment
    return (field[None], lam[None])


def split(value):
    hi = value.astype(jnp.bfloat16)
    return hi, (value - hi.astype(jnp.float32)).astype(jnp.bfloat16)


def stencil(scal, field, north, south):
    width = field.shape[1]
    east = pltpu.roll(field, width - 1, 1)
    west = pltpu.roll(field, 1, 1)
    return (
        field
        - scal[0] * field * (east - west) * 0.5
        - scal[1] * (north - south) * 0.5
        + scal[2] * (east + west + north + south - 4.0 * field)
    )


def weight_of(here_ref):
    def pick(number):
        value = WEIGHTS[0][number]
        for window in range(1, len(WEIGHTS)):
            value = jnp.where(here_ref[1] == window, WEIGHTS[window][number], value)
        return value

    return pick


def windowed(sign, share, own, ended):
    half = own.shape[1] // 2
    values = (ended, sign * ended + share * own)
    return [part for value in values for part in
            (value[:, :half] + value[:, half:], value[:, :half] - value[:, half:])]


def forecast_kernel(bands, here_ref, model, inside_ref, outside_ref, x_hbm, mult_hbm, x_ref, own_ref, x1_ref, *refs):
    outs, (ext, mid, mult_ref, sems) = refs[:4], refs[4:]
    band = x_ref.shape[0]
    edge = inside_ref.shape[0] // 2
    chunk = band // 4
    weight, scal = weight_of(here_ref), (model[0], model[1], model[2])
    sign, share, kept = weight(SIGN), weight(SHARE), weight(OWN)
    copies = []
    for number, (source, target, start) in enumerate(((x_hbm, ext, ROWS), (mult_hbm, mult_ref, 0))):
        for part in range(4):
            to = slice(start + part * chunk, start + (part + 1) * chunk)
            copies.append(pltpu.make_async_copy(
                source.at[part * chunk:(part + 1) * chunk], target.at[to], sems.at[number, part]
            ))
            copies[-1].start()

    def step(source, at, count):
        return stencil(scal, source[at:at + count], source[at + 1:at + count + 1], source[at - 1:at + count - 1])

    second_of_pair = lax.rem(here_ref[0], 2) == 1
    ext[ROWS - edge:ROWS] = jnp.where(second_of_pair, inside_ref[edge:], outside_ref[edge:])
    ext[ROWS + band:ROWS + band + edge] = jnp.where(second_of_pair, outside_ref[:edge], inside_ref[:edge])
    stepped = ROWS
    for part in range(4):
        copies[part].wait()
        if part == 0:
            mid[ROWS - 1:ROWS] = step(ext, ROWS - 1, 1) * jnp.where(here_ref[0] > 0, 1.0, 0.0)
        while stepped + ROWS < ROWS + (part + 1) * chunk or (part == 3 and stepped < ROWS + band):
            mid[stepped:stepped + ROWS] = step(ext, stepped, ROWS)
            stepped += ROWS
    mid[ROWS + band:ROWS + band + 1] = step(ext, ROWS + band, 1) * jnp.where(here_ref[0] < bands - 1, 1.0, 0.0)
    for part in range(4):
        copies[4 + part].wait()
        for at in range(part * chunk, (part + 1) * chunk, ROWS):
            rows, shifted = slice(at, at + ROWS), slice(at + ROWS, at + 2 * ROWS)
            field = ext[shifted]
            own = mult_ref[rows] + kept * field
            x_ref[rows], own_ref[rows], x1_ref[rows] = field, own, mid[shifted]
            for out, value in zip(outs, windowed(sign, share, own, 0.5 * step(mid, at + ROWS, ROWS))):
                out[rows] = value


def forecast(here, bands, model, x, mult, rims):
    band, width = x.shape
    whole = jax.ShapeDtypeStruct((band, width), jnp.float32)
    tall = pltpu.VMEM((band + 2 * ROWS, width), jnp.float32)
    return pl.pallas_call(
        functools.partial(forecast_kernel, bands),
        out_shape=[whole] * 3 + [jax.ShapeDtypeStruct((band, width // 2), jnp.float32)] * 4,
        in_specs=[SMEM] * 2 + [VMEM] * 2 + [HBM] * 2,
        out_specs=[VMEM] * 7,
        scratch_shapes=[tall, tall, pltpu.VMEM((band, width), jnp.float32), pltpu.SemaphoreType.DMA((2, 4))],
        compiler_params=LIMIT,
        cost_estimate=pl.CostEstimate(flops=40 * band * width, bytes_accessed=20 * band * width, transcendentals=0),
        name="forecast",
    )(here, model, *rims, *[pltpu.with_memory_space_constraint(value, pltpu.HBM) for value in (x, mult)])


def defect_kernel(here_ref, own_ref, obs_ref, mask_ref, x1_ref, plus_ref, minus_ref,
                  base_plus, base_minus, step_plus, second_ref, third_ref):
    half = own_ref.shape[1] // 2
    weight = weight_of(here_ref)
    first, share = weight(FIRST) > 0.0, weight(SHARE)
    for at in range(0, own_ref.shape[0], ROWS):
        rows = slice(at, at + ROWS)
        plus, minus = plus_ref[rows], minus_ref[rows]
        base, own = [], []
        for cols, end in ((slice(0, half), plus + minus), (slice(half, 2 * half), plus - minus)):
            own.append(own_ref[rows, cols])
            seen = mask_ref[:, rows, cols].astype(jnp.float32)
            base.append(
                own[-1] + seen[0] * (obs_ref[0, rows, cols] - x1_ref[rows, cols])
                + seen[1] * (obs_ref[1, rows, cols] - end)
            )
        base_plus[rows] = base[0] + base[1]
        base_minus[rows] = base[0] - base[1]
        own_plus, own_minus = own[0] + own[1], own[0] - own[1]
        step_plus[rows] = own_plus - plus
        sent_minus = minus + share * own_minus
        second_ref[rows] = jnp.where(first, plus + share * own_plus, sent_minus)
        third_ref[rows] = jnp.where(first, sent_minus, own_minus - minus)


def defect(here, own, obs, mask, x1, plus, minus):
    band, width = own.shape
    rows = 4 * ROWS
    whole = pl.BlockSpec((rows, width), lambda i: (i, 0))
    pair = pl.BlockSpec((2, rows, width), lambda i: (0, i, 0))
    part = pl.BlockSpec((rows, width // 2), lambda i: (i, 0))
    return pl.pallas_call(
        defect_kernel,
        grid=(band // rows,),
        out_shape=[jax.ShapeDtypeStruct((band, width // 2), jnp.float32)] * 5,
        in_specs=[SMEM, whole, pair, pair, whole, part, part],
        out_specs=[part] * 5,
        compiler_params=LIMIT,
        cost_estimate=pl.CostEstimate(flops=30 * band * width, bytes_accessed=40 * band * width, transcendentals=0),
        name="defect",
    )(here, own, obs, mask, x1, plus, minus)


def mix_kernel(first, here_ref, one_ref, other_ref, out_ref):
    weight = weight_of(here_ref)
    one = one_ref[...] if first is None else weight(first) * one_ref[...]
    out_ref[...] = one + weight(ONWARD if first is None else SIDE) * other_ref[...]


def mix(here, first, one, other):
    return pl.pallas_call(
        functools.partial(mix_kernel, first),
        out_shape=jax.ShapeDtypeStruct(one.shape, jnp.float32),
        in_specs=[SMEM] + [VMEM] * 2,
        out_specs=VMEM,
        compiler_params=LIMIT,
        cost_estimate=pl.CostEstimate(flops=3 * one.size, bytes_accessed=12 * one.size, transcendentals=0),
        name="mix",
    )(here, one, other)


def resid_kernel(bands, first, here_ref, base_ref, *refs):
    terms, outs = refs[:-bands], refs[-bands:]
    weights = [weight_of(here_ref)(first + number) for number in range(len(terms))]
    columns = outs[0].shape[1]
    for shift in range(bands):
        target = jnp.bitwise_xor(here_ref[0], shift)
        at = pl.ds(pl.multiple_of(target * columns, columns), columns)
        value = base_ref[:, at]
        for weight, term in zip(weights, terms):
            value = value - weight * term[:, at]
        outs[shift][...] = value


def resid_blocks(here, bands, first, base, *terms):
    band, half = base.shape
    columns = half // bands
    return pl.pallas_call(
        functools.partial(resid_kernel, bands, first),
        out_shape=[jax.ShapeDtypeStruct((band, columns), jnp.float32)] * bands,
        in_specs=[SMEM] + [VMEM] * 4,
        out_specs=[VMEM] * bands,
        compiler_params=LIMIT,
        cost_estimate=pl.CostEstimate(flops=8 * band * half, bytes_accessed=24 * band * half, transcendentals=0),
        name="resid_blocks",
    )(here, base, *terms)


def lat_kernel(bands, here_ref, *refs):
    blocks, (ehi, elo, ohi, olo) = refs[:bands], refs[bands:bands + 4]
    outs, (gathered, mixed) = refs[bands + 4:2 * bands + 4], refs[2 * bands + 4:]
    here = here_ref[0]
    pairs = bands // 2
    band, columns = blocks[0].shape
    for shift in range(pairs):
        source = jnp.bitwise_xor(here, shift)
        rows = pl.ds(pl.multiple_of(lax.rem(source, pairs) * band, band), band)
        first, other = blocks[shift][...], blocks[shift + pairs][...]
        sign = jnp.where(source < pairs, 1.0, -1.0)
        for part, value in enumerate((first + other, (first - other) * sign)):
            hi, lo = split(value)
            gathered[part, rows, :columns] = hi
            gathered[part, rows, columns:] = lo
    dot = functools.partial(jnp.dot, preferred_element_type=jnp.float32)
    for part, (hi, lo) in enumerate(((ehi, elo), (ohi, olo))):
        both = dot(hi[...], gathered[part])
        mixed[part] = both[:, :columns] + both[:, columns:] + dot(lo[...], gathered[part, :, :columns])
    for shift in range(bands):
        target = jnp.bitwise_xor(here, shift)
        rows = pl.ds(pl.multiple_of(lax.rem(target, pairs) * band, band), band)
        sign = jnp.where(target < pairs, 1.0, -1.0)
        outs[shift][...] = mixed[0, rows] + sign * mixed[1, rows]


def lat_apply(here, blocks, matrices):
    bands = len(blocks)
    band, columns = blocks[0].shape
    half = matrices[0].shape[0]
    return pl.pallas_call(
        functools.partial(lat_kernel, bands),
        out_shape=[jax.ShapeDtypeStruct((band, columns), jnp.float32)] * bands,
        in_specs=[SMEM] + [VMEM] * (bands + 4),
        out_specs=[VMEM] * bands,
        scratch_shapes=[
            pltpu.VMEM((2, half, 2 * columns), jnp.bfloat16),
            pltpu.VMEM((2, half, columns), jnp.float32),
        ],
        compiler_params=LIMIT,
        cost_estimate=pl.CostEstimate(
            flops=12 * half * half * columns, bytes_accessed=8 * half * half, transcendentals=0
        ),
        name="lat_apply",
    )(here, *blocks, *matrices)


def gather_rows(here, bands, blocks, gathered):
    band, columns = blocks[0].shape
    for shift in range(bands):
        source = jnp.bitwise_xor(here, shift)
        at = pl.ds(pl.multiple_of(source * columns, columns), columns)
        hi, lo = split(blocks[shift][...])
        gathered[:band, at] = hi
        gathered[band:, at] = lo


def lon_product(band, hi, lo, gathered):
    dot = functools.partial(jnp.dot, preferred_element_type=jnp.float32)
    both = dot(gathered[...], hi[...])
    return both[:band] + both[band:] + dot(gathered[:band], lo[...])


def lon_even_kernel(bands, here_ref, *refs):
    blocks, (hi, lo, out, gathered) = refs[:bands], refs[bands:]
    gather_rows(here_ref[0], bands, blocks, gathered)
    out[...] = lon_product(blocks[0].shape[0], hi, lo, gathered)


def lon_odd_kernel(bands, here_ref, *refs):
    blocks, (hi, lo, even, field, out, gathered, result, sems) = refs[:bands], refs[bands:]
    gather_rows(here_ref[0], bands, blocks, gathered)
    half = hi.shape[0]
    band, parts = blocks[0].shape[0], sems.shape[0]
    chunk = half // parts
    copies = []
    for part in range(parts):
        cols = slice(part * chunk, (part + 1) * chunk)
        odd = lon_product(band, hi.at[:, cols], lo.at[:, cols], gathered)
        for side, value in enumerate((even[:, cols] + odd, even[:, cols] - odd)):
            at = slice(side * half + part * chunk, side * half + (part + 1) * chunk)
            result[:, at] = field[:, at] + 0.5 * value
            copies.append(pltpu.make_async_copy(result.at[:, at], out.at[:, at], sems.at[part, side]))
            copies[-1].start()
    for copy in copies:
        copy.wait()


def lon_apply(here, blocks, matrices, extra=()):
    bands = len(blocks)
    band, _ = blocks[0].shape
    half = matrices[0].shape[0]
    scratch = [pltpu.VMEM((2 * band, half), jnp.bfloat16)]
    if extra:
        scratch += [pltpu.VMEM((band, 2 * half), jnp.float32), pltpu.SemaphoreType.DMA((4, 2))]
    return pl.pallas_call(
        functools.partial(lon_odd_kernel if extra else lon_even_kernel, bands),
        out_shape=jax.ShapeDtypeStruct((band, 2 * half if extra else half), jnp.float32),
        in_specs=[SMEM] + [VMEM] * (bands + 2 + len(extra)),
        out_specs=ANY if extra else VMEM,
        scratch_shapes=scratch,
        compiler_params=LIMIT,
        cost_estimate=pl.CostEstimate(
            flops=6 * band * half * half, bytes_accessed=4 * half * half, transcendentals=0
        ),
        name="lon_apply",
    )(here, *blocks, *matrices, *extra)


def multiplier_kernel(here_ref, own_ref, plus_ref, minus_ref, near_ref, direct_ref, out_ref, result, sems):
    known = weight_of(here_ref)(KNOWN)
    band, half = plus_ref.shape
    chunk = band // sems.shape[0]
    copies = []
    for at in range(0, band, ROWS):
        rows = slice(at, at + ROWS)
        plus, minus = plus_ref[rows] + known * (direct_ref[rows] - near_ref[rows]), minus_ref[rows]
        result[rows, :half] = own_ref[rows, :half] - 0.5 * (plus + minus)
        result[rows, half:] = own_ref[rows, half:] - 0.5 * (plus - minus)
        if (at + ROWS) % chunk == 0:
            part = slice(at + ROWS - chunk, at + ROWS)
            copies.append(pltpu.make_async_copy(result.at[part], out_ref.at[part], sems.at[at // chunk]))
            copies[-1].start()
    for copy in copies:
        copy.wait()


def new_multipliers(here, own, *terms):
    band, width = own.shape
    return pl.pallas_call(
        multiplier_kernel,
        out_shape=jax.ShapeDtypeStruct((band, width), jnp.float32),
        in_specs=[SMEM] + [VMEM] * 5,
        out_specs=ANY,
        scratch_shapes=[pltpu.VMEM((band, width), jnp.float32), pltpu.SemaphoreType.DMA((4,))],
        compiler_params=LIMIT,
        cost_estimate=pl.CostEstimate(flops=6 * band * width, bytes_accessed=20 * band * width, transcendentals=0),
        name="new_multipliers",
    )(here, own, *terms)


def exchange(blocks):
    bands = len(blocks)
    moved = list(blocks)
    for shift in [*range(bands // 2, bands), *range(2, bands // 2), 1]:
        route = [(source, source ^ shift) for source in range(bands)]
        moved[shift] = lax.ppermute(blocks[shift], "lat", route)
    return moved


def hop(value, pairs):
    return lax.ppermute(value, "win", pairs)


def per_device(
    state, multipliers, observations, obs_mask, speed, drift, kappa, lat_spectrum, lon_spectrum
):
    bands, windows = lax.axis_size("lat"), lax.axis_size("win")
    band, nlon = state.shape[2:]
    columns = nlon // 2 // bands
    if windows != 4 or state.shape[1] != 1 or bands & (bands - 1) or band % LANES or columns % LANES:
        return per_device_any(
            state, multipliers, observations, obs_mask, speed, drift, kappa, lat_spectrum, lon_spectrum
        )
    return per_device_hops(
        state, multipliers, observations, obs_mask, speed, drift, kappa, lat_spectrum, lon_spectrum
    )


def per_device_hops(
    state, multipliers, observations, obs_mask, speed, drift, kappa, lat_spectrum, lon_spectrum
):
    bands = lax.axis_size("lat")
    here = jnp.stack([lax.axis_index("lat"), lax.axis_index("win")]).astype(jnp.int32)
    x, mult = state[0, 0], multipliers[0, 0]
    rims = jnp.concatenate([x[:2], x[-2:]])
    edges = (
        lax.ppermute(rims, "lat", [(i, i ^ 1) for i in range(bands)]),
        lax.ppermute(rims, "lat", [pair for i in range(1, bands - 1, 2) for pair in ((i, i + 1), (i + 1, i))]),
    )
    x, own, x1, plus, minus, near, side = forecast(here, bands, jnp.concatenate([speed, drift, kappa]), x, mult, edges)
    near = hop(near, [(0, 1), (1, 0), (2, 3)])
    side = hop(side, [(0, 2), (1, 3)])
    base_plus, base_minus, step_plus, second, third = defect(
        here, own, observations[0, :, 0], obs_mask[0], x1, plus, minus
    )
    direct = hop(second, [(0, 1)])
    far = hop(mix(here, None, near, step_plus), [(0, 2), (1, 3)])
    cross = hop(mix(here, SECOND, second, side), [(2, 3), (3, 2)])
    third = hop(third, [(0, 1), (1, 3)])
    plus = hop(plus, [(1, 2), (2, 3)])
    minus = hop(minus, [(0, 1), (1, 2), (2, 3)])
    lat_matrices = build(lat_spectrum)
    lon_matrices = build(lon_spectrum)
    even = resid_blocks(here, bands, EVEN, base_plus, near, far, direct)
    odd = resid_blocks(here, bands, ODD, base_minus, side, cross, third)
    even, odd = exchange(even), exchange(odd)
    even = lat_apply(here, even, lat_matrices)
    even, odd = exchange(even), exchange(lat_apply(here, odd, lat_matrices))
    even = lon_apply(here, even, lon_matrices[:2])
    field = lon_apply(here, odd, lon_matrices[2:], (even, x))
    lam = new_multipliers(here, own, plus, minus, near, direct)
    return (field[None, None], lam[None, None])


def solution(mesh):
    return jax.shard_map(
        per_device,
        mesh=mesh,
        in_specs=(
            P("win", None, "lat", None),
            P("win", None, "lat", None),
            P("win", None, None, "lat", None),
            P("win", None, "lat", None),
            P(),
            P(),
            P(),
            P(),
            P(),
        ),
        out_specs=(P("win", None, "lat", None), P("win", None, "lat", None)),
        check_vma=False,
    )
```

```python
import functools
import math

import numpy as np
import jax
import jax.numpy as jnp
from jax import lax
from jax.experimental import pallas as pl
from jax.experimental.pallas import tpu as pltpu
from jax.sharding import PartitionSpec as P


LANES = 128
ROWS = 8
WEIGHTS = (
    (0.0, 1.0, -1.0, 1.0, 0.5, 1.0, 0.0, 0.0, 0.0, 0.0, 0.0, 0.0, 0.0, 0.0),
    (0.5, 1 / 2, 1.0, 0.0, 1.0, 0.0, 0.0, 0.0, 0.0, 1.0, 0.0, 0.0, 1.0, 0.5),
    (0.5, 1 / 3, 1.0, 0.0, 0.0, 1.0, 1 / 3, 0.0, 1.0, 0.0, 0.5, 1.0, 0.0, 0.0),
    (0.5, 1 / 4, 1.0, 0.0, 0.0, 0.0, 1.0, 1.0, 1 / 3, 0.0, 0.0, 1.0, 1 / 3, 0.0),
)
OWN, SHARE, SIGN, FIRST, ONWARD, SECOND, SIDE, EVEN, ODD, KNOWN = 0, 1, 2, 3, 4, 5, 6, 7, 10, 13
VMEM = pl.BlockSpec(memory_space=pltpu.VMEM)
SMEM = pl.BlockSpec(memory_space=pltpu.SMEM)
ANY = pl.BlockSpec(memory_space=pl.ANY)
HBM = pl.BlockSpec(memory_space=pltpu.HBM)
LIMIT = pltpu.CompilerParams(vmem_limit_bytes=16 * 2**20)


def trig_tables(count):
    low = count // LANES
    blocks = low // 2
    turn = 2.0 * math.pi
    fine = np.arange(LANES)
    coarse = np.arange(low)
    inner = turn * ((coarse[:, None] * fine[None, :]) % low) / low
    middle = turn * (((fine // low)[:, None] * fine[None, :]) % LANES) / LANES
    member = (coarse[:, None] == (fine % low)[None, :]).astype(np.float32)
    twist = turn * (coarse[:, None] * fine[None, :]) / count
    outer = turn * ((np.arange(blocks)[:, None] * coarse[None, :]) % low) / low
    even = (coarse % 2 == 0)[None, :]
    keep = np.concatenate([np.broadcast_to(even, outer.shape), np.broadcast_to(~even, outer.shape)])
    outer = np.concatenate([outer, outer])
    pack = lambda angle, scale: np.concatenate([np.cos(angle), np.sin(angle)], axis=1) * scale
    return (pack(inner, 1.0).astype(np.float32), pack(middle, 1.0).astype(np.float32), member, pack(twist, 1.0 / count).astype(np.float32),
            (np.cos(outer) * keep).astype(np.float32), (np.sin(outer) * keep).astype(np.float32))


def build_kernel(count, d_ref, inner_ref, middle_ref, member_ref, twist_ref, cos_ref, sin_ref, even_hi, even_lo, odd_hi, odd_lo, toep, hank):
    blocks = count // LANES // 2
    high = lax.Precision.HIGHEST
    mm = functools.partial(jnp.dot, precision=high, preferred_element_type=jnp.float32)

    def turned(value, table):
        real, imag = value[:, :LANES], value[:, LANES:]
        tc, ts = table[:, :LANES], table[:, LANES:]
        return jnp.concatenate([real * tc - imag * ts, real * ts + imag * tc], axis=1)

    spectrum = jnp.concatenate([d_ref[:, at:at + LANES] for at in range(0, count, LANES)], axis=0)
    g = lax.dot_general(spectrum, inner_ref[...], (((0,), (0,)), ((), ())), precision=high,
                        preferred_element_type=jnp.float32)
    g = turned(mm(member_ref[...], turned(g, middle_ref)), twist_ref)
    gc, gs = g[:, :LANES], g[:, LANES:]
    c = mm(cos_ref[...], gc) - mm(sin_ref[...], gs)
    s = mm(sin_ref[...], gc) + mm(cos_ref[...], gs)
    upside_down = ROWS - 1 - lax.broadcasted_iota(jnp.int32, (ROWS, LANES), 0)
    ahead = (lax.broadcasted_iota(jnp.int32, (LANES, LANES), 1)
             - lax.broadcasted_iota(jnp.int32, (LANES, LANES), 0))
    for part in range(2):
        wrap = 1.0 if part == 0 else -1.0
        hi_ref, lo_ref = (even_hi, even_lo) if part == 0 else (odd_hi, odd_lo)

        def sheared(table, at, shift):
            at += part * blocks
            return pltpu.roll(jnp.broadcast_to(table[at:at + 1], (LANES, LANES)), shift, 1, stride=1, stride_axis=0)

        before = wrap * sheared(c, blocks - 1, 0)
        for b in range(blocks):
            now = sheared(c, b, 0)
            block = jnp.where(ahead >= 0, now, before)
            toep[b] = block
            toep[b + blocks] = wrap * block
            before = now
        first = now = sheared(s, 0, 1)
        for b in range(blocks):
            after = sheared(s, b + 1, 1) if b + 1 < blocks else wrap * first
            block = jnp.where(ahead <= 0, now, after)
            for at in range(0, LANES, ROWS):
                rows = jnp.take_along_axis(block[at:at + ROWS], upside_down, axis=0)
                hank[b, LANES - ROWS - at:LANES - at] = rows
                hank[b + blocks, LANES - ROWS - at:LANES - at] = wrap * rows
            now = after

        def body(i, _):
            for j in range(blocks):
                a = toep[jnp.where(j < i, j - i + 2 * blocks, j - i)] + hank[i + j]
                hi = a.astype(jnp.bfloat16)
                at = (pl.ds(pl.multiple_of(i * LANES, LANES), LANES), pl.ds(j * LANES, LANES))
                hi_ref[at] = hi
                lo_ref[at] = (a - hi.astype(jnp.float32)).astype(jnp.bfloat16)
            return 0

        lax.fori_loop(0, blocks, body, 0)


def build(spectrum):
    count = spectrum.shape[1]
    half = count // 2
    tables = trig_tables(count)
    shape = jax.ShapeDtypeStruct((half, half), jnp.bfloat16)
    return pl.pallas_call(
        functools.partial(build_kernel, count),
        out_shape=[shape] * 4, in_specs=[VMEM] * 7, out_specs=[VMEM] * 4,
        scratch_shapes=[pltpu.VMEM((2 * half // LANES, LANES, LANES), jnp.float32)] * 2,
        compiler_params=LIMIT,
        cost_estimate=pl.CostEstimate(flops=2 * half * half * 8, bytes_accessed=8 * half * half, transcendentals=0),
    )(spectrum, *tables)


def extended(block, sides, width):
    for axis, dim in sides:
        count = lax.axis_size(axis)
        forward = [(i, i + 1) for i in range(count - 1)]
        backward = [(target, source) for source, target in forward]
        low = lax.ppermute(
            lax.slice_in_dim(block, block.shape[dim] - width, None, axis=dim), axis, forward
        )
        high = lax.ppermute(lax.slice_in_dim(block, 0, width, axis=dim), axis, backward)
        block = jnp.concatenate([low, block, high], axis=dim)
    return block


def passed_along(value, axis, steps):
    count = lax.axis_size(axis)
    first, last = (max(0, -steps), min(count, count - steps))
    return lax.ppermute(value, axis, [(source, source + steps) for source in range(first, last)])


def prefix(array, axis, combine, identity):
    peers, here = (lax.axis_size(axis), lax.axis_index(axis))
    everything = lax.all_gather(array, axis)
    start = jnp.broadcast_to(jnp.asarray(identity, array.dtype), array.shape)

    def turn(k, before):
        reached = k < here
        new = combine(before, everything[k])
        return jnp.where(reached, new, before)

    return lax.fori_loop(0, peers, turn, start)


def hartley(count):
    index = jnp.arange(count, dtype=jnp.int32)
    product = index[:, None] * index[None, :] % count
    angle = product.astype(jnp.float32) * (2.0 * math.pi / count)
    return jnp.cos(angle) + jnp.sin(angle)


def advance(padded, speed, drift, kappa):
    field = padded[:, 1:-1]
    north = padded[:, 2:]
    south = padded[:, :-2]
    east = jnp.roll(field, -1, axis=-1)
    west = jnp.roll(field, 1, axis=-1)
    speed_c = speed[:, None, None]
    drift_c = drift[:, None, None]
    kappa_c = kappa[:, None, None]
    return (
        field
        - speed_c * field * (east - west) * 0.5
        - drift_c * (north - south) * 0.5
        + kappa_c * (east + west + north + south - 4.0 * field)
    )


def per_device_any(
    state, multipliers, observations, obs_mask, speed, drift, kappa, lat_spectrum, lon_spectrum
):
    high = lax.Precision.HIGHEST
    field = state[0]
    lam = multipliers[0]
    observed = observations[0]
    mask = obs_mask[0].astype(jnp.float32)
    band = field.shape[1]
    nlon = field.shape[2]
    bands = lax.axis_size("lat")
    nlat = band * bands
    columns = nlon // bands
    lat_index = lax.axis_index("lat")
    win_index = lax.axis_index("win")
    h_lon = hartley(nlon)
    h_lat = hartley(nlat)
    lon_part = lax.dynamic_slice_in_dim(lon_spectrum, lat_index * columns, columns, 1)
    weight = lat_spectrum[:, :, None] * lon_part[:, None, :]
    divisor = jnp.maximum(win_index, 1).astype(jnp.float32)
    rows_global = lat_index * band + jnp.arange(-1, band + 1, dtype=jnp.int32)
    inside = ((rows_global >= 0) & (rows_global < nlat))[None, :, None]
    padded = extended(field, (("lat", 1),), 2)
    widened = advance(padded, speed, drift, kappa)
    widened = jnp.where(inside, widened, jnp.float32(0.0))
    first = widened[:, 1:-1]
    second = advance(widened, speed, drift, kappa)
    defect = mask[0][None] * (observed[0] - first) + mask[1][None] * (observed[1] - second)
    prior_end = passed_along(second, "win", 1)
    mismatch = jnp.where(win_index > 0, field - prior_end, jnp.float32(0.0))
    lam = lam + 0.5 * mismatch
    carried = prefix(lam, "win", lambda earlier, later: earlier + later, jnp.zeros_like(lam))
    resid = defect + lam - carried / divisor
    spectral = jnp.matmul(resid, h_lon, precision=high)
    spectral = lax.all_to_all(spectral, "lat", split_axis=2, concat_axis=1, tiled=True)
    spectral = jnp.einsum("ij,ljk->lik", h_lat, spectral, precision=high) * weight
    spectral = jnp.einsum("ij,ljk->lik", h_lat, spectral, precision=high)
    spectral = lax.all_to_all(spectral, "lat", split_axis=1, concat_axis=2, tiled=True)
    increment = jnp.matmul(spectral, h_lon, precision=high) / (nlat * nlon)
    field = field + 0.5 * increment
    return (field[None], lam[None])


def split(value):
    hi = value.astype(jnp.bfloat16)
    return hi, (value - hi.astype(jnp.float32)).astype(jnp.bfloat16)


def stencil(scal, field, north, south):
    width = field.shape[1]
    east = pltpu.roll(field, width - 1, 1)
    west = pltpu.roll(field, 1, 1)
    return (
        field
        - scal[0] * field * (east - west) * 0.5
        - scal[1] * (north - south) * 0.5
        + scal[2] * (east + west + north + south - 4.0 * field)
    )


def weight_of(here_ref):
    def pick(number):
        value = WEIGHTS[0][number]
        for window in range(1, len(WEIGHTS)):
            value = jnp.where(here_ref[1] == window, WEIGHTS[window][number], value)
        return value

    return pick


def windowed(sign, share, own, ended):
    half = own.shape[1] // 2
    values = (ended, sign * ended + share * own)
    return [part for value in values for part in
            (value[:, :half] + value[:, half:], value[:, :half] - value[:, half:])]


def forecast_kernel(bands, here_ref, model, inside_ref, outside_ref, x_hbm, mult_hbm, x_ref, own_ref, x1_ref, *refs):
    outs, (ext, mid, mult_ref, sems) = refs[:4], refs[4:]
    band = x_ref.shape[0]
    edge = inside_ref.shape[0] // 2
    chunk = band // 4
    weight, scal = weight_of(here_ref), (model[0], model[1], model[2])
    sign, share, kept = weight(SIGN), weight(SHARE), weight(OWN)
    copies = []
    for number, (source, target, start) in enumerate(((x_hbm, ext, ROWS), (mult_hbm, mult_ref, 0))):
        for part in range(4):
            to = slice(start + part * chunk, start + (part + 1) * chunk)
            copies.append(pltpu.make_async_copy(
                source.at[part * chunk:(part + 1) * chunk], target.at[to], sems.at[number, part]
            ))
            copies[-1].start()

    def step(source, at, count):
        return stencil(scal, source[at:at + count], source[at + 1:at + count + 1], source[at - 1:at + count - 1])

    second_of_pair = lax.rem(here_ref[0], 2) == 1
    ext[ROWS - edge:ROWS] = jnp.where(second_of_pair, inside_ref[edge:], outside_ref[edge:])
    ext[ROWS + band:ROWS + band + edge] = jnp.where(second_of_pair, outside_ref[:edge], inside_ref[:edge])
    stepped = ROWS
    for part in range(4):
        copies[part].wait()
        if part == 0:
            mid[ROWS - 1:ROWS] = step(ext, ROWS - 1, 1) * jnp.where(here_ref[0] > 0, 1.0, 0.0)
        while stepped + ROWS < ROWS + (part + 1) * chunk or (part == 3 and stepped < ROWS + band):
            mid[stepped:stepped + ROWS] = step(ext, stepped, ROWS)
            stepped += ROWS
    mid[ROWS + band:ROWS + band + 1] = step(ext, ROWS + band, 1) * jnp.where(here_ref[0] < bands - 1, 1.0, 0.0)
    for part in range(4):
        copies[4 + part].wait()
        for at in range(part * chunk, (part + 1) * chunk, ROWS):
            rows, shifted = slice(at, at + ROWS), slice(at + ROWS, at + 2 * ROWS)
            field = ext[shifted]
            own = mult_ref[rows] + kept * field
            x_ref[rows], own_ref[rows], x1_ref[rows] = field, own, mid[shifted]
            for out, value in zip(outs, windowed(sign, share, own, 0.5 * step(mid, at + ROWS, ROWS))):
                out[rows] = value


def forecast(here, bands, model, x, mult, rims):
    band, width = x.shape
    whole = jax.ShapeDtypeStruct((band, width), jnp.float32)
    tall = pltpu.VMEM((band + 2 * ROWS, width), jnp.float32)
    return pl.pallas_call(
        functools.partial(forecast_kernel, bands),
        out_shape=[whole] * 3 + [jax.ShapeDtypeStruct((band, width // 2), jnp.float32)] * 4,
        in_specs=[SMEM] * 2 + [VMEM] * 2 + [HBM] * 2,
        out_specs=[VMEM] * 7,
        scratch_shapes=[tall, tall, pltpu.VMEM((band, width), jnp.float32), pltpu.SemaphoreType.DMA((2, 4))],
        compiler_params=LIMIT,
        cost_estimate=pl.CostEstimate(flops=40 * band * width, bytes_accessed=20 * band * width, transcendentals=0),
        name="forecast",
    )(here, model, *rims, *[pltpu.with_memory_space_constraint(value, pltpu.HBM) for value in (x, mult)])


def defect_kernel(here_ref, own_ref, obs_ref, mask_ref, x1_ref, plus_ref, minus_ref,
                  base_plus, base_minus, step_plus, second_ref, third_ref):
    half = own_ref.shape[1] // 2
    weight = weight_of(here_ref)
    first, share = weight(FIRST) > 0.0, weight(SHARE)
    for at in range(0, own_ref.shape[0], ROWS):
        rows = slice(at, at + ROWS)
        plus, minus = plus_ref[rows], minus_ref[rows]
        base, own = [], []
        for cols, end in ((slice(0, half), plus + minus), (slice(half, 2 * half), plus - minus)):
            own.append(own_ref[rows, cols])
            seen = mask_ref[:, rows, cols].astype(jnp.float32)
            base.append(
                own[-1] + seen[0] * (obs_ref[0, rows, cols] - x1_ref[rows, cols])
                + seen[1] * (obs_ref[1, rows, cols] - end)
            )
        base_plus[rows] = base[0] + base[1]
        base_minus[rows] = base[0] - base[1]
        own_plus, own_minus = own[0] + own[1], own[0] - own[1]
        step_plus[rows] = own_plus - plus
        sent_minus = minus + share * own_minus
        second_ref[rows] = jnp.where(first, plus + share * own_plus, sent_minus)
        third_ref[rows] = jnp.where(first, sent_minus, own_minus - minus)


def defect(here, own, obs, mask, x1, plus, minus):
    band, width = own.shape
    rows = 4 * ROWS
    whole = pl.BlockSpec((rows, width), lambda i: (i, 0))
    pair = pl.BlockSpec((2, rows, width), lambda i: (0, i, 0))
    part = pl.BlockSpec((rows, width // 2), lambda i: (i, 0))
    return pl.pallas_call(
        defect_kernel,
        grid=(band // rows,),
        out_shape=[jax.ShapeDtypeStruct((band, width // 2), jnp.float32)] * 5,
        in_specs=[SMEM, whole, pair, pair, whole, part, part],
        out_specs=[part] * 5,
        compiler_params=LIMIT,
        cost_estimate=pl.CostEstimate(flops=30 * band * width, bytes_accessed=40 * band * width, transcendentals=0),
        name="defect",
    )(here, own, obs, mask, x1, plus, minus)


def mix_kernel(first, here_ref, one_ref, other_ref, out_ref):
    weight = weight_of(here_ref)
    one = one_ref[...] if first is None else weight(first) * one_ref[...]
    out_ref[...] = one + weight(ONWARD if first is None else SIDE) * other_ref[...]


def mix(here, first, one, other):
    return pl.pallas_call(
        functools.partial(mix_kernel, first),
        out_shape=jax.ShapeDtypeStruct(one.shape, jnp.float32),
        in_specs=[SMEM] + [VMEM] * 2,
        out_specs=VMEM,
        compiler_params=LIMIT,
        cost_estimate=pl.CostEstimate(flops=3 * one.size, bytes_accessed=12 * one.size, transcendentals=0),
        name="mix",
    )(here, one, other)


def resid_kernel(bands, first, here_ref, base_ref, *refs):
    terms, outs = refs[:-bands], refs[-bands:]
    weights = [weight_of(here_ref)(first + number) for number in range(len(terms))]
    columns = outs[0].shape[1]
    for shift in range(bands):
        target = jnp.bitwise_xor(here_ref[0], shift)
        at = pl.ds(pl.multiple_of(target * columns, columns), columns)
        value = base_ref[:, at]
        for weight, term in zip(weights, terms):
            value = value - weight * term[:, at]
        outs[shift][...] = value


def resid_blocks(here, bands, first, base, *terms):
    band, half = base.shape
    columns = half // bands
    return pl.pallas_call(
        functools.partial(resid_kernel, bands, first),
        out_shape=[jax.ShapeDtypeStruct((band, columns), jnp.float32)] * bands,
        in_specs=[SMEM] + [VMEM] * 4,
        out_specs=[VMEM] * bands,
        compiler_params=LIMIT,
        cost_estimate=pl.CostEstimate(flops=8 * band * half, bytes_accessed=24 * band * half, transcendentals=0),
        name="resid_blocks",
    )(here, base, *terms)


def lat_kernel(bands, here_ref, *refs):
    blocks, (ehi, elo, ohi, olo) = refs[:bands], refs[bands:bands + 4]
    outs, (gathered, mixed) = refs[bands + 4:2 * bands + 4], refs[2 * bands + 4:]
    here = here_ref[0]
    pairs = bands // 2
    band, columns = blocks[0].shape
    for shift in range(pairs):
        source = jnp.bitwise_xor(here, shift)
        rows = pl.ds(pl.multiple_of(lax.rem(source, pairs) * band, band), band)
        first, other = blocks[shift][...], blocks[shift + pairs][...]
        sign = jnp.where(source < pairs, 1.0, -1.0)
        for part, value in enumerate((first + other, (first - other) * sign)):
            hi, lo = split(value)
            gathered[part, rows, :columns] = hi
            gathered[part, rows, columns:] = lo
    dot = functools.partial(jnp.dot, preferred_element_type=jnp.float32)
    for part, (hi, lo) in enumerate(((ehi, elo), (ohi, olo))):
        both = dot(hi[...], gathered[part])
        mixed[part] = both[:, :columns] + both[:, columns:] + dot(lo[...], gathered[part, :, :columns])
    for shift in range(bands):
        target = jnp.bitwise_xor(here, shift)
        rows = pl.ds(pl.multiple_of(lax.rem(target, pairs) * band, band), band)
        sign = jnp.where(target < pairs, 1.0, -1.0)
        outs[shift][...] = mixed[0, rows] + sign * mixed[1, rows]


def lat_apply(here, blocks, matrices):
    bands = len(blocks)
    band, columns = blocks[0].shape
    half = matrices[0].shape[0]
    return pl.pallas_call(
        functools.partial(lat_kernel, bands),
        out_shape=[jax.ShapeDtypeStruct((band, columns), jnp.float32)] * bands,
        in_specs=[SMEM] + [VMEM] * (bands + 4),
        out_specs=[VMEM] * bands,
        scratch_shapes=[
            pltpu.VMEM((2, half, 2 * columns), jnp.bfloat16),
            pltpu.VMEM((2, half, columns), jnp.float32),
        ],
        compiler_params=LIMIT,
        cost_estimate=pl.CostEstimate(
            flops=12 * half * half * columns, bytes_accessed=8 * half * half, transcendentals=0
        ),
        name="lat_apply",
    )(here, *blocks, *matrices)


def gather_rows(places, blocks, gathered):
    band, columns = blocks[0].shape
    for place, block in zip(places, blocks):
        at = pl.ds(pl.multiple_of(place * columns, columns), columns)
        hi, lo = split(block[...])
        gathered[:band, at] = hi
        gathered[band:, at] = lo


def lon_product(band, hi, lo, gathered):
    dot = functools.partial(jnp.dot, preferred_element_type=jnp.float32)
    both = dot(gathered[...], hi)
    return both[:band] + both[band:] + dot(gathered[:band], lo)


def lon_even_kernel(here_ref, *refs):
    blocks, (hi, lo, out, gathered) = refs[:-4], refs[-4:]
    gather_rows([jnp.bitwise_xor(here_ref[0], shift) for shift in range(len(blocks))], blocks, gathered)
    out[...] = lon_product(blocks[0].shape[0], hi[...], lo[...], gathered)


def lon_half(here, count, far):
    half = jnp.bitwise_and(here, count)
    first = count - half if far else half
    return [jnp.bitwise_xor(jnp.bitwise_and(here, count - 1), shift) for shift in range(count)], first


def lon_near_kernel(here_ref, *refs):
    blocks, (hi, lo, out, gathered) = refs[:-4], refs[-4:]
    band, columns = blocks[0].shape
    places, first = lon_half(here_ref[0], len(blocks), False)
    gather_rows(places, blocks, gathered)
    rows = pl.ds(pl.multiple_of(first * columns, columns), len(blocks) * columns)
    out[...] = lon_product(band, hi[rows], lo[rows], gathered)


def lon_far_kernel(here_ref, *refs):
    blocks, (hi, lo, even, near, field, out, gathered, result, sems) = refs[:-9], refs[-9:]
    band, columns = blocks[0].shape
    places, first = lon_half(here_ref[0], len(blocks), True)
    gather_rows(places, blocks, gathered)
    rows = pl.ds(pl.multiple_of(first * columns, columns), len(blocks) * columns)
    half, parts = hi.shape[0], sems.shape[0]
    chunk = half // parts
    copies = []
    for part in range(parts):
        cols = slice(part * chunk, (part + 1) * chunk)
        odd = near[:, cols] + lon_product(band, hi[rows, cols], lo[rows, cols], gathered)
        for side, value in enumerate((even[:, cols] + odd, even[:, cols] - odd)):
            at = slice(side * half + part * chunk, side * half + (part + 1) * chunk)
            result[:, at] = field[:, at] + 0.5 * value
            copies.append(pltpu.make_async_copy(result.at[:, at], out.at[:, at], sems.at[part, side]))
            copies[-1].start()
    for copy in copies:
        copy.wait()


def lon_apply(kernel, here, blocks, matrices, extra=()):
    band, columns = blocks[0].shape
    half = matrices[0].shape[0]
    depth = len(blocks) * columns
    scratch = [pltpu.VMEM((2 * band, depth), jnp.bfloat16)]
    if extra:
        scratch += [pltpu.VMEM((band, 2 * half), jnp.float32), pltpu.SemaphoreType.DMA((4, 2))]
    return pl.pallas_call(
        kernel,
        out_shape=jax.ShapeDtypeStruct((band, 2 * half if extra else half), jnp.float32),
        in_specs=[SMEM] + [VMEM] * (len(blocks) + 2 + len(extra)),
        out_specs=ANY if extra else VMEM,
        scratch_shapes=scratch,
        compiler_params=LIMIT,
        cost_estimate=pl.CostEstimate(
            flops=6 * band * depth * half, bytes_accessed=4 * depth * half, transcendentals=0
        ),
        name="lon_apply",
    )(here, *blocks, *matrices, *extra)


def multiplier_kernel(here_ref, own_ref, plus_ref, minus_ref, near_ref, direct_ref, out_ref, result, sems):
    known = weight_of(here_ref)(KNOWN)
    band, half = plus_ref.shape
    chunk = band // sems.shape[0]
    copies = []
    for at in range(0, band, ROWS):
        rows = slice(at, at + ROWS)
        plus, minus = plus_ref[rows] + known * (direct_ref[rows] - near_ref[rows]), minus_ref[rows]
        result[rows, :half] = own_ref[rows, :half] - 0.5 * (plus + minus)
        result[rows, half:] = own_ref[rows, half:] - 0.5 * (plus - minus)
        if (at + ROWS) % chunk == 0:
            part = slice(at + ROWS - chunk, at + ROWS)
            copies.append(pltpu.make_async_copy(result.at[part], out_ref.at[part], sems.at[at // chunk]))
            copies[-1].start()
    for copy in copies:
        copy.wait()


def new_multipliers(here, own, *terms):
    band, width = own.shape
    return pl.pallas_call(
        multiplier_kernel,
        out_shape=jax.ShapeDtypeStruct((band, width), jnp.float32),
        in_specs=[SMEM] + [VMEM] * 5,
        out_specs=ANY,
        scratch_shapes=[pltpu.VMEM((band, width), jnp.float32), pltpu.SemaphoreType.DMA((4,))],
        compiler_params=LIMIT,
        cost_estimate=pl.CostEstimate(flops=6 * band * width, bytes_accessed=20 * band * width, transcendentals=0),
        name="new_multipliers",
    )(here, own, *terms)


def exchange(blocks):
    bands = len(blocks)
    moved = list(blocks)
    for shift in [*range(bands // 2, bands), *range(2, bands // 2), 1]:
        route = [(source, source ^ shift) for source in range(bands)]
        moved[shift] = lax.ppermute(blocks[shift], "lat", route)
    return moved


def hop(value, pairs):
    return lax.ppermute(value, "win", pairs)


def per_device(
    state, multipliers, observations, obs_mask, speed, drift, kappa, lat_spectrum, lon_spectrum
):
    bands, windows = lax.axis_size("lat"), lax.axis_size("win")
    band, nlon = state.shape[2:]
    columns = nlon // 2 // bands
    if windows != 4 or state.shape[1] != 1 or bands & (bands - 1) or band % LANES or columns % LANES:
        return per_device_any(
            state, multipliers, observations, obs_mask, speed, drift, kappa, lat_spectrum, lon_spectrum
        )
    return per_device_hops(
        state, multipliers, observations, obs_mask, speed, drift, kappa, lat_spectrum, lon_spectrum
    )


def per_device_hops(
    state, multipliers, observations, obs_mask, speed, drift, kappa, lat_spectrum, lon_spectrum
):
    bands = lax.axis_size("lat")
    here = jnp.stack([lax.axis_index("lat"), lax.axis_index("win")]).astype(jnp.int32)
    x, mult = state[0, 0], multipliers[0, 0]
    rims = jnp.concatenate([x[:2], x[-2:]])
    edges = (
        lax.ppermute(rims, "lat", [pair for i in range(1, bands - 1, 2) for pair in ((i, i + 1), (i + 1, i))]),
        lax.ppermute(rims, "lat", [(i, i ^ 1) for i in range(bands)]),
    )[::-1]
    x, own, x1, plus, minus, near, side = forecast(here, bands, jnp.concatenate([speed, drift, kappa]), x, mult, edges)
    near = hop(near, [(0, 1), (1, 0), (2, 3)])
    side = hop(side, [(0, 2), (1, 3)])
    base_plus, base_minus, step_plus, second, third = defect(
        here, own, observations[0, :, 0], obs_mask[0], x1, plus, minus
    )
    direct = hop(second, [(0, 1)])
    far = hop(mix(here, None, near, step_plus), [(0, 2), (1, 3)])
    cross = hop(mix(here, SECOND, second, side), [(2, 3), (3, 2)])
    third = hop(third, [(0, 1), (1, 3)])
    plus = hop(plus, [(1, 2), (2, 3)])
    minus = hop(minus, [(0, 1), (1, 2), (2, 3)])
    lat_matrices = build(lat_spectrum)
    lon_matrices = build(lon_spectrum)
    even = resid_blocks(here, bands, EVEN, base_plus, near, far, direct)
    odd = resid_blocks(here, bands, ODD, base_minus, side, cross, third)
    even, odd = exchange(even), exchange(odd)
    even = lat_apply(here, even, lat_matrices)
    odd = lat_apply(here, odd, lat_matrices)
    even, odd = exchange(even), exchange(odd)
    even = lon_apply(lon_even_kernel, here, even, lon_matrices[:2])
    near_odd = lon_apply(lon_near_kernel, here, odd[:bands // 2], lon_matrices[2:])
    field = lon_apply(lon_far_kernel, here, odd[bands // 2:], lon_matrices[2:], (even, near_odd, x))
    lam = new_multipliers(here, own, plus, minus, near, direct)
    return (field[None, None], lam[None, None])


def solution(mesh):
    return jax.shard_map(
        per_device,
        mesh=mesh,
        in_specs=(
            P("win", None, "lat", None),
            P("win", None, "lat", None),
            P("win", None, None, "lat", None),
            P("win", None, "lat", None),
            P(),
            P(),
            P(),
            P(),
            P(),
        ),
        out_specs=(P("win", None, "lat", None), P("win", None, "lat", None)),
        check_vma=False,
    )
```
